32 devices in a mesh: dp: 4 (over y, core), expert: 8 (over z, x).
Axes of the slice: x: 2, y: 2, z: 4, core: 2. Of those that a mesh axis runs over, the one named last changes fastest.
Arguments:
- hidden_in: bfloat16 [2048, 2048], P(('dp', 'expert')), may hold values from -6 to 6
- context: bfloat16 [2048, 2048], P(('dp', 'expert')), may hold values from -6 to 6
- out_proj: bfloat16 [2048, 2048], P(('dp', 'expert')), may hold values from -0.125 to 0.125
- norm_gain: float32 [2048], replicated, may hold values from 0.5 to 1.5
- router: bfloat16 [2048, 64], P(('dp', 'expert')), may hold values from -0.25 to 0.25
- expert_ids: int32 [2048, 8], P(('dp', 'expert')), may hold values from 0 to 63, as said below
- replica_expert: int32 [128], replicated, may hold values from 0 to 63, as said below
- split_pick: int32 [2048, 8], P(('dp', 'expert')), may hold values from 0 to 65535
- up_gate: bfloat16 [128, 2048, 2048], P(('dp', 'expert')), may hold values from -0.125 to 0.125
- down: bfloat16 [128, 1024, 2048], P(('dp', 'expert')), may hold values from -0.1875 to 0.1875
Outputs:
- layer_out: bfloat16 [2048, 2048], P(('dp', 'expert'))
The draws below stay inside these ranges and needn't reach their ends.
Inputs may be any that keep to these rules, and one draw needn't show every extreme that they name: `expert_ids`: each row names 8 different experts. `replica_expert`: every expert is served by one replica or more.
All inputs are finite; a program needn't handle non-finite values.
Results may differ from the reference program's by a relative error of at most 0.004.
Values may be sent and summed in bfloat16 or wider, within the bound.
A program may use at most 128 MiB of HBM per device.

```python
import jax
import jax.numpy as jnp
from jax import lax

D = 2048
FF = 1024
EXPERTS = 64
TOPK = 8
HOT = 16
TOK_DEV = 64
REPLICAS = 128
TOKENS = 2048
CAP = 8
DEVICES = 32


def expert_order(key):
    return jax.random.permutation(jax.random.fold_in(key, 101), EXPERTS).astype(jnp.int32)


def draw_replica_expert(key, part):
    order_list = expert_order(key)
    hot_list = order_list[:HOT]
    extras = hot_list[jnp.arange(REPLICAS - EXPERTS, dtype=jnp.int32) % HOT]
    listing = jnp.concatenate([jnp.arange(EXPERTS, dtype=jnp.int32), extras.astype(jnp.int32)])
    shuffle = jax.random.permutation(jax.random.fold_in(key, 102), REPLICAS)
    return listing[shuffle].astype(jnp.int32)


def draw_expert_ids(key, part):
    order_list = expert_order(key)
    hot_list = order_list[:HOT]
    cold_list = order_list[HOT:]
    hot_scores = jax.random.randint(jax.random.fold_in(key, 103), (TOKENS, HOT), 0, 1 << 20) * HOT + jnp.arange(HOT, dtype=jnp.int32)[None, :]
    cold_scores = jax.random.randint(jax.random.fold_in(key, 104), (TOKENS, EXPERTS - HOT), 0, 1 << 20) * (EXPERTS - HOT) + jnp.arange(EXPERTS - HOT, dtype=jnp.int32)[None, :]
    hot_top = lax.top_k(hot_scores, TOPK)[1]
    cold_top = lax.top_k(cold_scores, 2)[1]
    hot_ids = hot_list[hot_top]
    cold_ids = cold_list[cold_top]
    hot_number = TOPK - 2 + jax.random.randint(jax.random.fold_in(key, 105), (TOKENS, 1), 0, 2)
    column = jnp.arange(TOPK, dtype=jnp.int32)[None, :]
    cold_pick = jnp.clip(column - hot_number, 0, 1)
    from_cold = jnp.take_along_axis(cold_ids, cold_pick, axis=1)
    return jnp.where(column < hot_number, hot_ids, from_cold).astype(jnp.int32)


def set_ends(result, stream_key, low, top_value):
    longest = result.shape.index(max(result.shape))
    spots = []
    for shift in (0, 1):
        where = [jax.random.randint(jax.random.fold_in(stream_key, axis), (), 0, length) for axis, length in enumerate(result.shape)]
        where[longest] = (where[longest] + shift) % result.shape[longest]
        spots.append(tuple(where))
    return result.at[spots[0]].set(low).at[spots[1]].set(top_value)


def block_scale(own_key, extent, cuts, low, largest):
    factor_of, own = 1.0, jax.random.fold_in(own_key, 6)
    for axis_at, shards_of in cuts:
        heights = jnp.exp(jax.random.uniform(jax.random.fold_in(own, axis_at), (shards_of,), jnp.float32, low / len(cuts), largest / len(cuts)))
        factor_of = factor_of * jnp.repeat(heights, extent[axis_at] // shards_of).reshape([-1 if axis == axis_at else 1 for axis in range(len(extent))])
    return factor_of


def bell_draw(stream_key, dims, spread, most, shards=(), kind=jnp.bfloat16):
    array = spread * jax.random.normal(stream_key, dims, jnp.float32)
    if shards:
        array = array * block_scale(stream_key, dims, shards, -0.22, 0.18)
    return jnp.clip(array, -most, most).astype(kind)


def setup_inputs(seed: int = 0) -> dict:
    key_of = jax.random.split(jax.random.key(seed), 11)
    return {
        "hidden_in": bell_draw(key_of[0], (TOKENS, D), 1.0, 6.0, ((0, 32),)),
        "context": bell_draw(key_of[1], (TOKENS, D), 1.0, 6.0, ((0, 32),)),
        "out_proj": bell_draw(key_of[2], (D, D), D ** -0.5, 0.125, ((0, 32),)),
        "norm_gain": jnp.clip(1.0 + 0.1 * jax.random.normal(key_of[3], (D,), jnp.float32), 0.5, 1.5),
        "router": bell_draw(key_of[4], (D, EXPERTS), (D // 4) ** -0.5, 0.25, ((0, 32),)),
        "expert_ids": draw_expert_ids(jax.random.fold_in(key_of[10], 71), 0),
        "replica_expert": draw_replica_expert(jax.random.fold_in(key_of[10], 71), 0),
        "split_pick": set_ends(jax.random.randint(key_of[7], (TOKENS, TOPK), 0, 65536), jax.random.fold_in(key_of[7], 1), 0, 65535).astype(jnp.int32),
        "up_gate": bell_draw(key_of[8], (REPLICAS, D, 2 * FF), D ** -0.5, 0.125, ((0, 32),)),
        "down": bell_draw(key_of[9], (REPLICAS, FF, D), FF ** -0.5, 0.1875, ((0, 32),)),
    }


def rms_norm(residual, norm_gain):
    scale_back = lax.rsqrt(lax.optimization_barrier(jnp.mean(residual * residual, axis=-1, keepdims=True)) + 1e-05)
    return (residual * scale_back * norm_gain).astype(jnp.bfloat16)

def route_block(expert_ids, split_pick, replica_expert):
    replica_total = replica_expert.shape[0]
    replica_iota = lax.iota(jnp.int32, replica_total)
    same_expert = replica_expert[:, None] == replica_expert[None, :]
    earlier = replica_iota[:, None] > replica_iota[None, :]
    replica_rank = lax.optimization_barrier(jnp.sum((same_expert & earlier).astype(jnp.int32), axis=1)).astype(jnp.int32)
    serves = expert_ids[:, :, None] == replica_expert[None, None, :]
    replica_count = lax.optimization_barrier(jnp.sum(serves.astype(jnp.int32), axis=-1)).astype(jnp.int32)
    wanted = (split_pick % replica_count).astype(jnp.int32)
    matches = serves & (replica_rank[None, None, :] == wanted[:, :, None])
    replica = lax.optimization_barrier(jnp.sum(jnp.where(matches, replica_iota[None, None, :], 0), axis=-1)).astype(jnp.int32)
    flat_replica = replica.reshape(-1)
    pair_iota = lax.iota(jnp.int32, flat_replica.shape[0])
    same_target = flat_replica[:, None] == flat_replica[None, :]
    before = pair_iota[:, None] > pair_iota[None, :]
    slot_index = lax.optimization_barrier(jnp.sum((same_target & before).astype(jnp.int32), axis=1)).astype(jnp.int32)
    return (replica, slot_index.reshape(replica.shape))

def reference(hidden_in, context, out_proj, norm_gain, router, expert_ids, replica_expert, split_pick, up_gate, down):
    projected = jnp.dot(context, out_proj, preferred_element_type=jnp.float32)
    residual = hidden_in.astype(jnp.float32) + projected
    normed = rms_norm(residual, norm_gain)
    logits = jnp.dot(normed, router, preferred_element_type=jnp.float32)
    chosen = jnp.take_along_axis(logits, expert_ids, axis=1)
    raised = jnp.exp(chosen)
    route_weight = raised / lax.optimization_barrier(jnp.sum(raised, axis=-1, keepdims=True))

    def route_pair(inputs):
        return route_block(inputs[0], inputs[1], replica_expert)
    id_blocks = expert_ids.reshape(DEVICES, TOK_DEV, TOPK)
    pick_blocks = split_pick.reshape(DEVICES, TOK_DEV, TOPK)
    replica, slot_index = lax.map(route_pair, (id_blocks, pick_blocks))
    within_cap = slot_index < CAP
    source = lax.iota(jnp.int32, DEVICES)[:, None, None]
    token_index = source * TOK_DEV + lax.iota(jnp.int32, TOK_DEV)[None, :, None]
    token_index = jnp.broadcast_to(token_index, replica.shape).astype(jnp.int32)
    slot_count = DEVICES * CAP
    position = jnp.where(within_cap, replica * slot_count + source * CAP + slot_index, REPLICAS * slot_count).astype(jnp.int32)
    anchor_table = jnp.full((REPLICAS * slot_count,), -1, jnp.int32)
    anchor_table = anchor_table.at[position.reshape(-1)].set(token_index.reshape(-1), mode='drop')
    weight_table = jnp.zeros((REPLICAS * slot_count,), jnp.float32)
    weight_table = weight_table.at[position.reshape(-1)].set(route_weight.reshape(-1), mode='drop')
    anchor_table = anchor_table.reshape(REPLICAS, slot_count)
    weight_table = weight_table.reshape(REPLICAS, slot_count)

    def expert_step(summed, inputs_slice):
        anchor_row, slot_weight, replica_up, replica_down = inputs_slice
        has_row = anchor_row >= 0
        safe_index = jnp.maximum(anchor_row, 0).astype(jnp.int32)
        expert_in = jnp.where(has_row[:, None], normed[safe_index], jnp.zeros((), jnp.bfloat16))
        gate_up = jnp.dot(expert_in, replica_up, preferred_element_type=jnp.float32)
        hidden_act = (jax.nn.silu(gate_up[:, :FF]) * gate_up[:, FF:]).astype(jnp.bfloat16)
        expert_out = jnp.dot(hidden_act, replica_down, preferred_element_type=jnp.float32).astype(jnp.bfloat16)
        summed = summed.at[safe_index].add(slot_weight[:, None] * expert_out.astype(jnp.float32))
        return (summed, None)
    final = lax.scan(expert_step, residual, (anchor_table, weight_table, up_gate, down))[0]
    return final.astype(jnp.bfloat16)
```

```python
import functools

import jax
import jax.numpy as jnp
from jax import lax
from jax.experimental import pallas as pl
from jax.experimental.pallas import tpu as pltpu
from jax.sharding import PartitionSpec as P


def rms_norm(residual, norm_gain):
    scale_back = lax.rsqrt(jnp.mean(residual * residual, axis=-1, keepdims=True) + 1e-05)
    return (residual * scale_back * norm_gain).astype(jnp.bfloat16)


def route_block(expert_ids, split_pick, replica_expert):
    replica_total = replica_expert.shape[0]
    replica_iota = lax.iota(jnp.int32, replica_total)
    same_expert = replica_expert[:, None] == replica_expert[None, :]
    earlier = replica_iota[:, None] > replica_iota[None, :]
    replica_rank = jnp.sum((same_expert & earlier).astype(jnp.int32), axis=1)
    serves = expert_ids[:, :, None] == replica_expert[None, None, :]
    replica_count = jnp.sum(serves.astype(jnp.int32), axis=-1)
    wanted = split_pick % replica_count
    matches = serves & (replica_rank[None, None, :] == wanted[:, :, None])
    replica = jnp.sum(jnp.where(matches, replica_iota[None, None, :], 0), axis=-1)
    flat_replica = replica.reshape(-1)
    pair_iota = lax.iota(jnp.int32, flat_replica.shape[0])
    same_target = flat_replica[:, None] == flat_replica[None, :]
    before = pair_iota[:, None] > pair_iota[None, :]
    slot_index = jnp.sum((same_target & before).astype(jnp.int32), axis=1)
    return (replica, slot_index.reshape(replica.shape))


def apply_experts(incoming, up_gate, down, capacity):
    arrived_shape = incoming.shape
    local_reps = up_gate.shape[0]
    hidden_units = down.shape[1]
    stacked = incoming.reshape(-1, local_reps, capacity, incoming.shape[-1])
    gate_up = jnp.einsum("sjcd,jdf->sjcf", stacked, up_gate, preferred_element_type=jnp.float32)
    hidden_act = (jax.nn.silu(gate_up[..., :hidden_units]) * gate_up[..., hidden_units:]).astype(
        jnp.bfloat16
    )
    expert_out = jnp.einsum("sjcf,jfd->sjcd", hidden_act, down, preferred_element_type=jnp.float32)
    return expert_out.astype(jnp.bfloat16).reshape(arrived_shape)


def per_device(
    hidden_in,
    context,
    out_proj,
    norm_gain,
    router,
    expert_ids,
    replica_expert,
    split_pick,
    up_gate,
    down,
):
    tok_rows, model_width = hidden_in.shape
    top_count = expert_ids.shape[1]
    replica_total = replica_expert.shape[0]
    local_reps = up_gate.shape[0]
    data_groups = lax.axis_size("dp")
    expert_groups = lax.axis_size("expert")
    capacity = max(2, 2 * tok_rows * top_count // replica_total)
    summed = jnp.dot(
        context,
        lax.all_gather(out_proj, ("dp", "expert"), axis=0, tiled=True),
        preferred_element_type=jnp.float32,
    )
    router_rows = lax.all_gather(router, ("dp", "expert"), axis=0, tiled=True)
    residual = hidden_in.astype(jnp.float32) + summed
    normed = rms_norm(residual, norm_gain)
    logits = jnp.dot(normed, router_rows, preferred_element_type=jnp.float32)
    hit_mask = expert_ids[:, :, None] == lax.iota(jnp.int32, logits.shape[1])[None, None, :]
    chosen = jnp.sum(jnp.where(hit_mask, logits[:, None, :], 0.0), axis=-1)
    raised = jnp.exp(chosen)
    route_weight = raised / jnp.sum(raised, axis=-1, keepdims=True)
    replica, slot_index = route_block(expert_ids, split_pick, replica_expert)
    within_cap = slot_index < capacity
    buffer_row = jnp.where(within_cap, replica * capacity + slot_index, -1).reshape(-1)
    slot_total = replica_total * capacity
    matches = buffer_row[None, :] == lax.iota(jnp.int32, slot_total)[:, None]
    filled = jnp.any(matches, axis=1)
    row_of_pair = lax.iota(jnp.int32, tok_rows * top_count) // top_count
    anchor = jnp.sum(jnp.where(matches, row_of_pair[None, :], 0), axis=1)
    outgoing = jnp.where(filled[:, None], normed[anchor], jnp.zeros((), jnp.bfloat16))
    outgoing = outgoing.reshape(data_groups, expert_groups, local_reps * capacity, model_width)
    incoming = lax.all_to_all(
        lax.all_to_all(outgoing, "expert", split_axis=1, concat_axis=1, tiled=True),
        "dp",
        split_axis=0,
        concat_axis=0,
        tiled=True,
    )
    results = apply_experts(incoming, up_gate, down, capacity)
    returned = lax.all_to_all(
        lax.all_to_all(results, "dp", split_axis=0, concat_axis=0, tiled=True),
        "expert",
        split_axis=1,
        concat_axis=1,
        tiled=True,
    )
    returned = returned.reshape(slot_total, model_width)
    safe_index = jnp.where(within_cap, replica * capacity + slot_index, 0)
    gathered = returned[safe_index]
    kept_weight = jnp.where(within_cap, route_weight, 0.0)
    layer_out = residual + jnp.sum(kept_weight[:, :, None] * gathered.astype(jnp.float32), axis=1)
    return layer_out.astype(jnp.bfloat16)

MESH = pl.DeviceIdType.MESH
LINE = 4
SIDE = 128
CHUNKS = 4
LAG = 2
DEEP = LAG * (LINE + 1)
RING = 4
DOWN_RING = 2
GROUP = 4


def place():
    d, e = lax.axis_index("dp"), lax.axis_index("expert")
    return d // 2, d % 2, e // 2, e % 2


def device_of(y, c, z, x):
    return (y * 2 + c, z * 2 + x)


def block_of(y, c, z, x):
    return (y * 2 + c) * (2 * LINE) + z * 2 + x


def greet(barrier, y, c, z, x):
    for other in (device_of(y, 1 - c, z, x), device_of(1 - y, c, z, x), device_of(y, c, z, 1 - x)):
        pl.semaphore_signal(barrier, inc=1, device_id=other, device_id_type=MESH)

    @pl.when(z > 0)
    def _():
        pl.semaphore_signal(barrier, inc=1, device_id=device_of(y, c, z - 1, x), device_id_type=MESH)

    @pl.when(z < LINE - 1)
    def _():
        pl.semaphore_signal(barrier, inc=1, device_id=device_of(y, c, z + 1, x), device_id_type=MESH)

    pl.semaphore_wait(barrier, 3 + jnp.minimum(z, 1) + jnp.minimum(LINE - 1 - z, 1))


def plane_shift(q, p):
    qa, qb = q & 1, q >> 1
    return qb * (1 - p) + qa * p, qa * (1 - p) + qb * p


def chunk_kind(k):
    turn = 3 * (k // 4) + (k % 4 + 1) // 2
    return k % 4 == 1, turn % 2


def side_kind(k):
    return k >= 0, k


def step_count(q, source_z, z):
    return LAG * (jnp.maximum(source_z - z, z - source_z) + (q & 1) + (q >> 1))


def remote(src, dst, send_sem, recv_sem, target):
    return pltpu.make_async_remote_copy(
        src_ref=src, dst_ref=dst, send_sem=send_sem, recv_sem=recv_sem, device_id=target, device_id_type=MESH
    )


class Spread:
    def __init__(self, chunks, where, kind, many, up_sem, down_sem, a_sem, b_sem, twin_sem, recv_sem, twin_recv):
        self.chunks, self.where, self.kind, self.many = chunks, where, kind, many
        self.up_sem, self.down_sem, self.a_sem, self.b_sem = up_sem, down_sem, a_sem, b_sem
        self.twin_sem, self.recv_sem, self.twin_recv = twin_sem, recv_sem, twin_recv
        self.pos = place()

    def sends(self, k, q, source_z, act):
        y, c, z, x = self.pos
        along_z, p = self.kind(k)
        dy, dx = plane_shift(q, p)
        item = self.where(k, block_of((y + dy) % 2, c, source_z, (x + dx) % 2))
        slot = q * LINE + source_z
        recv = self.recv_sem.at[k, ((dy + y) % 2) * 8 + source_z * 2 + (x + dx) % 2]
        line_on = True if q == 0 else along_z
        plane_on = jnp.logical_or(jnp.logical_not(along_z), z == source_z)

        @pl.when((z < LINE - 1) & (z >= source_z) & line_on)
        def _():
            act(remote(item, item, self.up_sem.at[k, slot], recv, device_of(y, c, z + 1, x)))

        @pl.when((z > 0) & (z <= source_z) & line_on)
        def _():
            act(remote(item, item, self.down_sem.at[k, slot], recv, device_of(y, c, z - 1, x)))

        if q == 0:
            @pl.when(plane_on)
            def _():
                act(remote(item, item, self.a_sem.at[k, source_z], recv, device_of((y + p) % 2, c, z, (x + 1 - p) % 2)))

        if q <= 1:
            @pl.when(plane_on)
            def _():
                act(remote(item, item, self.b_sem.at[k, slot], recv, device_of((y + 1 - p) % 2, c, z, (x + p) % 2)))

    def arrive(self, k, q, source_z):
        y, c, z, x = self.pos
        _, p = self.kind(k)
        dy, dx = plane_shift(q, p)
        item = self.where(k, block_of((y + dy) % 2, c, source_z, (x + dx) % 2))
        recv = self.recv_sem.at[k, ((dy + y) % 2) * 8 + source_z * 2 + (x + dx) % 2]
        remote(item, item, self.twin_sem.at[k, 0], recv, device_of(y, 1 - c, z, x)).wait_recv()

    def twin(self, k, half, core):
        y, c, z, x = self.pos
        items = self.many(k, half, core)
        return remote(items, items, self.twin_sem.at[k, half], self.twin_recv.at[k, half], device_of(y, 1 - c, z, x))

    def step(self, s):
        y, c, z, x = self.pos
        for source_z in range(LINE):
            for q in range(4):
                k = s - step_count(q, source_z, z)

                @pl.when((k >= 0) & (k < self.chunks))
                def _(q=q, source_z=source_z, k=k):
                    if q == 0:
                        @pl.when(z != source_z)
                        def _():
                            self.arrive(k, q, source_z)
                    else:
                        self.arrive(k, q, source_z)
                    self.sends(k, q, source_z, lambda copy: copy.start())

        k = s - DEEP

        @pl.when((k >= 0) & (k < self.chunks))
        def _():
            for half in range(2):
                self.twin(k, half, c).start()

    def ready(self, k):
        for half in range(2):
            self.twin(k, half, 1 - self.pos[1]).wait_recv()

    def drain(self):
        def body(k, carry):
            for source_z in range(LINE):
                for q in range(4):
                    self.sends(k, q, source_z, lambda copy: copy.wait_send())
            for half in range(2):
                self.twin(k, half, self.pos[1]).wait_send()
            return carry

        lax.fori_loop(0, self.chunks, body, 0)


def layer_kernel(
    plan, hid_ref, ctx_ref, proj_ref, gain_ref, router_ref, ids_ref, rep_ref, split_ref, up_ref, down_ref,
    out_ref, proj_buf, norm_buf, side_buf, weight_side, res_buf, up_ring, down_ring, acc_buf, act_buf, pick_buf,
    weight_buf, result_buf, core_buf, a_buf, b_buf, diag_buf, line_buf, line_end, hop_buf, local_sem, up_load,
    down_load, *sems
):
    tok_rows, width, top, capacity, reps, replica_total, expert_total, hidden_units, blocks = plan
    y, c, z, x = place()
    me = block_of(y, c, z, x)
    chunk = width // CHUNKS
    groups = blocks // GROUP
    group_rows = GROUP * tok_rows
    seats = GROUP * capacity
    slots = reps * seats
    unit = chunk
    units = width // unit
    f32, bf16 = jnp.float32, jnp.bfloat16

    def own_copy(k):
        return pltpu.make_async_copy(
            proj_ref.at[:, pl.ds(k * chunk, chunk)], proj_buf.at[k, me], local_sem.at[k]
        )

    def up_copy(i):
        u, j = i // reps, i % reps
        return pltpu.make_async_copy(
            up_ref.at[j, pl.ds(pl.multiple_of(u * unit, unit), unit)], up_ring.at[i % RING], up_load.at[i % RING]
        )

    def down_copy(k):
        return pltpu.make_async_copy(
            down_ref.at[:, :, pl.ds(pl.multiple_of(k * chunk, chunk), chunk)],
            down_ring.at[k % DOWN_RING],
            down_load.at[k % DOWN_RING],
        )

    for k in range(CHUNKS):
        own_copy(k).start()
    greet(pltpu.get_barrier_semaphore(), y, c, z, x)
    for i in range(RING):
        up_copy(i).start()
    for k in range(DOWN_RING):
        down_copy(k).start()

    def chunk_spread(buf, group):
        return Spread(
            CHUNKS, lambda k, b: buf.at[k, b], chunk_kind,
            lambda k, h, core: buf.at[k, pl.ds((h * 2 + core) * 8, 8)], *group,
        )

    def side_spread(buf, group):
        return Spread(
            1, lambda k, b: buf.at[b], side_kind, lambda k, h, core: buf.at[pl.ds((h * 2 + core) * 8, 8)], *group
        )

    first, second = chunk_spread(proj_buf, sems[0:7]), chunk_spread(norm_buf, sems[7:14])
    first_side, second_side = side_spread(side_buf, sems[14:21]), side_spread(weight_side, sems[21:28])
    twin_sem, twin_recv, hop_sem, a_recv, b_recv, diag_recv, line_recv, end_recv = sems[28:]

    for k in range(CHUNKS):
        own_copy(k).wait()
    first.step(0)

    rep_row = jnp.broadcast_to(rep_ref[...], (replica_total, replica_total))
    row_i = lax.broadcasted_iota(jnp.int32, (replica_total, replica_total), 0)
    col_i = lax.broadcasted_iota(jnp.int32, (replica_total, replica_total), 1)
    rep_col = jnp.sum(jnp.where(row_i == col_i, rep_row, 0), axis=1, keepdims=True)
    rank = jnp.sum(jnp.where((rep_row == rep_col) & (col_i < row_i), 1, 0), axis=1, keepdims=True)
    replica_i = lax.broadcasted_iota(jnp.int32, (replica_total, tok_rows), 0)
    taken = jnp.zeros((replica_total, tok_rows), f32)
    hits, replicas = [], []
    for k in range(top):
        serves = rep_col == ids_ref[k : k + 1, :]
        count = jnp.sum(jnp.where(serves, 1.0, 0.0), axis=0, keepdims=True)
        pick = split_ref[k : k + 1, :].astype(f32)
        wanted = pick - jnp.floor((pick + 0.5) / count) * count
        hit = serves & (rank.astype(f32) == wanted)
        hits.append(hit)
        taken = jnp.where(hit, 1.0, taken)
        replicas.append(jnp.sum(jnp.where(hit, replica_i, 0).astype(f32), axis=0, keepdims=True))
    tok_i = lax.broadcasted_iota(jnp.int32, (tok_rows, tok_rows), 0)
    tok_j = lax.broadcasted_iota(jnp.int32, (tok_rows, tok_rows), 1)
    before = jnp.where(tok_i < tok_j, 1.0, 0.0).astype(bf16)
    earlier = jnp.dot(taken.astype(bf16), before, preferred_element_type=f32)
    slot_rows = [
        jnp.minimum(jnp.sum(jnp.where(hit, earlier, 0.0), axis=0, keepdims=True), float(capacity)) for hit in hits
    ]
    wide_i = lax.broadcasted_iota(jnp.int32, (tok_rows, SIDE), 0)
    wide_j = lax.broadcasted_iota(jnp.int32, (tok_rows, SIDE), 1)
    widen = jnp.where(wide_j == wide_i + x * tok_rows, 1.0, 0.0).astype(bf16)
    routing = jnp.concatenate(replicas + slot_rows, axis=0).astype(bf16)
    side_buf[me, tok_rows:] = jnp.dot(routing, widen, preferred_element_type=f32).astype(bf16)
    spread_i = lax.broadcasted_iota(jnp.int32, (expert_total, SIDE), 0)
    spread_j = lax.broadcasted_iota(jnp.int32, (expert_total, SIDE), 1)
    side_buf[me, :tok_rows] = jnp.dot(
        router_ref[...], jnp.where(spread_i == spread_j, 1.0, 0.0).astype(bf16), preferred_element_type=f32
    ).astype(bf16)

    def project(k):
        first.ready(k)
        weights = proj_buf[k].reshape(width, chunk)
        summed = jnp.dot(ctx_ref[...], weights, preferred_element_type=f32)
        columns = pl.ds(pl.multiple_of(k * chunk, chunk), chunk)
        res_buf[k] = hid_ref[:, columns].astype(f32) + summed

    def first_body(s, carry):
        first.step(s)
        first_side.step(s - 1)
        k = s - (DEEP + 1)

        @pl.when((k >= 0) & (k < CHUNKS))
        def _():
            project(k)

        return carry

    lax.fori_loop(1, CHUNKS + DEEP + 1, first_body, 0)
    square = jnp.zeros((tok_rows, 1), f32)
    for k in range(CHUNKS):
        square += jnp.sum(res_buf[k] * res_buf[k], axis=1, keepdims=True)
    scale_back = lax.rsqrt(square / width + 1e-05)
    for k in range(CHUNKS):
        norm_buf[k, me] = (res_buf[k] * scale_back * gain_ref[:, k * chunk : (k + 1) * chunk]).astype(bf16)
    second.step(0)

    first_side.ready(0)
    logits = jnp.zeros((tok_rows, SIDE), f32)
    share = chunk // tok_rows
    for k in range(CHUNKS):
        rows = side_buf[k * share : (k + 1) * share, :tok_rows].reshape(chunk, SIDE)
        logits += jnp.dot(norm_buf[k, me], rows, preferred_element_type=f32)
    logits = logits.T
    expert_i = lax.broadcasted_iota(jnp.int32, (SIDE, tok_rows), 0)
    raised = [
        jnp.exp(jnp.sum(jnp.where(expert_i == ids_ref[k : k + 1, :], logits, 0.0), axis=0, keepdims=True))
        for k in range(top)
    ]
    raised = jnp.concatenate(raised, axis=0)
    route_weight = raised / jnp.sum(raised, axis=0, keepdims=True)
    upper = route_weight.astype(bf16).astype(f32)
    both = jnp.concatenate([upper, route_weight - upper], axis=0).astype(bf16)
    weight_side[me] = jnp.dot(both, widen, preferred_element_type=f32).astype(bf16)

    lane = lax.broadcasted_iota(jnp.int32, (1, group_rows), 1)
    slot_i = lax.broadcasted_iota(jnp.int32, (slots, group_rows), 0).astype(f32)
    seat_base = (lane // tok_rows * capacity).astype(f32)
    low = (me * reps).astype(f32)

    def group_side(ref, g, start, stop):
        def pair(i):
            return ref[GROUP * g + i, start:stop].astype(f32) + ref[GROUP * g + i + 1, start:stop].astype(f32)

        return jnp.concatenate([pair(0), pair(2)], axis=1)

    def seats_of(g):
        routed = group_side(side_buf, g, tok_rows, tok_rows + 2 * top)
        replica = routed[:top] - low
        slot = routed[top:]
        here = (replica >= 0) & (replica < reps) & (slot < capacity)
        return jnp.where(here, replica * seats + seat_base + slot, -1.0)

    def pick_body(g, carry):
        seat = seats_of(g)
        picked = jnp.zeros((slots, group_rows), f32)
        for k in range(top):
            picked = jnp.where(slot_i == seat[k : k + 1], 1.0, picked)
        pick_buf[g] = picked.astype(bf16)
        return carry

    def weigh_body(g, carry):
        seat = seats_of(g)
        weights = group_side(weight_side, g, 0, 2 * top)
        high = jnp.zeros((slots, group_rows), f32)
        rest = high
        for k in range(top):
            hit = slot_i == seat[k : k + 1]
            high = jnp.where(hit, weights[k : k + 1], high)
            rest = jnp.where(hit, weights[top + k : top + k + 1], rest)
        weight_buf[g, :, :slots] = high.T.astype(bf16)
        weight_buf[g, :, slots:] = rest.T.astype(bf16)
        return carry

    second.step(1)
    second_side.step(0)
    lax.fori_loop(0, groups, pick_body, 0)
    acc_buf[...] = jnp.zeros_like(acc_buf)

    def take(k):
        second.ready(k)

        def body(g, carry):
            rows = norm_buf[k, pl.ds(g * GROUP, GROUP)].reshape(group_rows, chunk)
            taken = jnp.dot(pick_buf[g], rows, preferred_element_type=f32).astype(bf16)
            for j in range(reps):
                act_buf[
                    (k % 2) * reps + j,
                    pl.ds(pl.multiple_of(g * seats, seats), seats),
                ] = taken[j * seats : (j + 1) * seats]
            return carry

        lax.fori_loop(0, groups, body, 0)

    def raise_some(u, start, stop):
        def body(j, carry):
            i = u * reps + j
            up_copy(i).wait()
            expert_in = act_buf[(u % 2) * reps + j]
            for t in range(4):
                columns = slice(t * (2 * hidden_units // 4), (t + 1) * (2 * hidden_units // 4))
                acc_buf[j, :, columns] += jnp.dot(
                    expert_in, up_ring[i % RING, :, columns], preferred_element_type=f32
                )

            @pl.when(i + RING < units * reps)
            def _():
                up_copy(i + RING).start()

            return carry

        lax.fori_loop(start, stop, body, 0)

    def second_body(s, carry):
        second.step(s)
        second_side.step(s - 1)
        k = s - (DEEP + 1)

        @pl.when(s == DEEP + 1)
        def _():
            second_side.ready(0)
            lax.fori_loop(0, groups, weigh_body, 0)

        @pl.when((k >= 0) & (k < CHUNKS))
        def _():
            take(k)
            raise_some(k, 0, reps)

        return carry

    lax.fori_loop(2, CHUNKS + DEEP + 1, second_body, 0)

    def act_body(j, carry):
        for h in range(2):
            half = hidden_units // 2
            gate = acc_buf[j, :, h * half : (h + 1) * half]
            raised = acc_buf[j, :, hidden_units + h * half : hidden_units + (h + 1) * half]
            act_buf[2 * j + h] = (gate / (1.0 + jnp.exp(-gate)) * raised).astype(bf16)
        return carry

    lax.fori_loop(0, reps, act_body, 0)
    first.drain()
    first_side.drain()

    def lower_chunk(k):
        down_copy(k).wait()
        for j in range(reps):
            half = hidden_units // 2
            result = jnp.dot(act_buf[2 * j], down_ring[k % DOWN_RING, j, :half], preferred_element_type=f32)
            result += jnp.dot(act_buf[2 * j + 1], down_ring[k % DOWN_RING, j, half:], preferred_element_type=f32)
            result = result.astype(bf16)
            for g in range(groups):
                some = result[g * seats : (g + 1) * seats]
                result_buf[g, j * seats : (j + 1) * seats] = some
                result_buf[g, slots + j * seats : slots + (j + 1) * seats] = some

        @pl.when(k + DOWN_RING < CHUNKS)
        def _():
            down_copy(k + DOWN_RING).start()

        def body(g, carry):
            summed = jnp.dot(weight_buf[g], result_buf[g], preferred_element_type=f32).astype(bf16)
            proj_buf[k, pl.ds(g * GROUP, GROUP)] = summed.reshape(GROUP, tok_rows, chunk)
            return carry

        lax.fori_loop(0, groups, body, 0)

    def to_twin(k, half):
        return remote(
            proj_buf.at[k, pl.ds((half * 2 + 1 - c) * 8, 8)],
            core_buf.at[k, pl.ds(half * 8, 8)],
            twin_sem.at[k, half],
            twin_recv.at[k, half],
            device_of(y, 1 - c, z, x),
        )

    def hop(k, q, target_z, act):
        along_z, p = chunk_kind(k)
        dy, dx = plane_shift(q, p)
        item = core_buf.at[k, ((y + dy) % 2) * 8 + target_z * 2 + (x + dx) % 2]
        sem = hop_sem.at[k, q * LINE + target_z]
        over_a = device_of((y + p) % 2, c, z, (x + 1 - p) % 2)
        over_b = device_of((y + 1 - p) % 2, c, z, (x + p) % 2)
        up, down = device_of(y, c, z + 1, x), device_of(y, c, z - 1, x)
        in_plane = jnp.logical_or(jnp.logical_not(along_z), z == target_z)
        off_plane = jnp.logical_not(in_plane) if q else z != target_z
        if q:
            @pl.when(in_plane)
            def _():
                if q == 1:
                    act(remote(item, a_buf.at[k, target_z], sem, a_recv.at[k, target_z], over_a))
                elif q == 2:
                    act(remote(item, b_buf.at[k, target_z], sem, b_recv.at[k, target_z], over_b))
                else:
                    act(remote(item, diag_buf.at[k, target_z], sem, diag_recv.at[k, target_z], over_b))

        @pl.when(off_plane & (target_z < z))
        def _():
            act(remote(item, line_buf.at[k, q, target_z], sem, line_recv.at[k, q * LINE + target_z], down))

        @pl.when(off_plane & (target_z > z + 1))
        def _():
            act(remote(item, line_buf.at[k, q, target_z], sem, line_recv.at[k, q * LINE + target_z], up))

        @pl.when(off_plane & (target_z == z + 1))
        def _():
            act(remote(item, line_end.at[k, q], sem, end_recv.at[k, q], up))

    def join(k, q, target_z):
        along_z, p = chunk_kind(k)
        dy, dx = plane_shift(q, p)
        y_to, x_to = (y + dy) % 2, (x + dx) % 2
        place_of = y_to * 8 + target_z * 2 + x_to
        in_plane = jnp.logical_or(jnp.logical_not(along_z), z == target_z)
        line_on = True if q == 0 else along_z
        hop_buf[...] = core_buf[k, place_of].astype(f32) + proj_buf[
            k, block_of(y_to, c, target_z, x_to)
        ].astype(f32)

        def add(ref, sem):
            remote(ref, ref, hop_sem.at[k, 0], sem, device_of(y, 1 - c, z, x)).wait_recv()
            hop_buf[...] += ref[...].astype(f32)

        if q == 1:
            @pl.when(in_plane)
            def _():
                add(diag_buf.at[k, target_z], diag_recv.at[k, target_z])

        if q == 0:
            @pl.when(in_plane)
            def _():
                add(a_buf.at[k, target_z], a_recv.at[k, target_z])
                add(b_buf.at[k, target_z], b_recv.at[k, target_z])

        @pl.when(((target_z <= z) & (z < LINE - 1) | (target_z > z) & (z > 0)) & line_on)
        def _():
            add(line_buf.at[k, q, target_z], line_recv.at[k, q * LINE + target_z])

        @pl.when((target_z == z) & (z > 0) & line_on)
        def _():
            add(line_end.at[k, q], end_recv.at[k, q])

        if q == 0:
            @pl.when(target_z == z)
            def _():
                columns = pl.ds(pl.multiple_of(k * chunk, chunk), chunk)
                out_ref[:, columns] = (res_buf[k] + hop_buf[...]).astype(bf16)

            @pl.when(target_z != z)
            def _():
                core_buf[k, place_of] = hop_buf[...].astype(bf16)
        else:
            core_buf[k, place_of] = hop_buf[...].astype(bf16)
        hop(k, q, target_z, lambda copy: copy.start())

    def third_body(s, carry):
        k = s - 1

        @pl.when((k >= 0) & (k < CHUNKS))
        def _():
            for half in range(2):
                to_twin(k, half).wait_recv()

        for q in (3, 1, 2, 0):
            for target_z in range(LINE):
                k = s - 1 - (DEEP - step_count(q, target_z, z))

                @pl.when((k >= 0) & (k < CHUNKS))
                def _(q=q, target_z=target_z, k=k):
                    join(k, q, target_z)

        @pl.when(s < CHUNKS)
        def _():
            lower_chunk(s)
            for half in range(2):
                to_twin(s, half).start()

        return carry

    lax.fori_loop(0, CHUNKS + DEEP + 1, third_body, 0)

    def last_body(k, carry):
        for half in range(2):
            to_twin(k, half).wait_send()
        for q in range(4):
            for target_z in range(LINE):
                hop(k, q, target_z, lambda copy: copy.wait_send())
        return carry

    lax.fori_loop(0, CHUNKS, last_body, 0)
    second.drain()
    second_side.drain()


def run_layer(
    hidden_in, context, out_proj, norm_gain, router, expert_ids, replica_expert, split_pick, up_gate, down
):
    tok_rows, width = hidden_in.shape
    top = expert_ids.shape[1]
    replica_total = replica_expert.shape[0]
    expert_total = router.shape[1]
    reps, hidden_units, _ = down.shape
    blocks = lax.axis_size("dp") * lax.axis_size("expert")
    capacity = max(2, 2 * tok_rows * top // replica_total)
    chunk = width // CHUNKS
    groups = blocks // GROUP
    seats = GROUP * capacity
    slots = reps * seats
    dma = pltpu.SemaphoreType.DMA
    vmem, anywhere = pl.BlockSpec(memory_space=pltpu.VMEM), pl.BlockSpec(memory_space=pl.ANY)

    def spread_sems(chunks):
        return [dma((chunks, 16)), dma((chunks, 16)), dma((chunks, LINE)), dma((chunks, 2 * LINE)), dma((chunks, 2)),
                dma((chunks, 16)), dma((chunks, 2))]

    bf16, f32 = jnp.bfloat16, jnp.float32
    plan = (tok_rows, width, top, capacity, reps, replica_total, expert_total, hidden_units, blocks)
    return pl.pallas_call(
        functools.partial(layer_kernel, plan),
        out_shape=jax.ShapeDtypeStruct((tok_rows, width), bf16),
        in_specs=[vmem, vmem, anywhere, vmem, vmem, vmem, vmem, vmem, anywhere, anywhere],
        out_specs=vmem,
        scratch_shapes=[
            pltpu.VMEM((CHUNKS, blocks, tok_rows, chunk), bf16),
            pltpu.VMEM((CHUNKS, blocks, tok_rows, chunk), bf16),
            pltpu.VMEM((blocks, tok_rows + 2 * top, SIDE), bf16),
            pltpu.VMEM((blocks, 2 * top, SIDE), bf16),
            pltpu.VMEM((CHUNKS, tok_rows, chunk), f32),
            pltpu.VMEM((RING, chunk, 2 * hidden_units), bf16),
            pltpu.VMEM((DOWN_RING, reps, hidden_units, chunk), bf16),
            pltpu.VMEM((reps, groups * seats, 2 * hidden_units), f32),
            pltpu.VMEM((2 * reps, groups * seats, hidden_units // 2), bf16),
            pltpu.VMEM((groups, slots, GROUP * tok_rows), bf16),
            pltpu.VMEM((groups, GROUP * tok_rows, 2 * slots), bf16),
            pltpu.VMEM((groups, 2 * slots, chunk), bf16),
            pltpu.VMEM((CHUNKS, blocks // 2, tok_rows, chunk), bf16),
            pltpu.VMEM((CHUNKS, LINE, tok_rows, chunk), bf16),
            pltpu.VMEM((CHUNKS, LINE, tok_rows, chunk), bf16),
            pltpu.VMEM((CHUNKS, LINE, tok_rows, chunk), bf16),
            pltpu.VMEM((CHUNKS, 4, LINE, tok_rows, chunk), bf16),
            pltpu.VMEM((CHUNKS, 4, tok_rows, chunk), bf16),
            pltpu.VMEM((tok_rows, chunk), f32),
            dma((CHUNKS,)),
            dma((RING,)),
            dma((DOWN_RING,)),
        ]
        + spread_sems(CHUNKS)
        + spread_sems(CHUNKS)
        + spread_sems(1)
        + spread_sems(1)
        + [
            dma((CHUNKS, 2)),
            dma((CHUNKS, 2)),
            dma((CHUNKS, 16)),
            dma((CHUNKS, LINE)),
            dma((CHUNKS, LINE)),
            dma((CHUNKS, LINE)),
            dma((CHUNKS, 16)),
            dma((CHUNKS, 4)),
        ],
        compiler_params=pltpu.CompilerParams(collective_id=0, has_side_effects=True, vmem_limit_bytes=62 << 20),
    )(
        hidden_in, context, out_proj, norm_gain.reshape(1, width), router, expert_ids.T,
        replica_expert.reshape(1, replica_total), split_pick.T, up_gate, down,
    )


def solution(mesh):
    plan = run_layer if (mesh.shape["dp"], mesh.shape["expert"]) == (4, 8) else per_device
    return jax.shard_map(
        plan,
        mesh=mesh,
        in_specs=(
            P(("dp", "expert"), None),
            P(("dp", "expert"), None),
            P(("dp", "expert"), None),
            P(),
            P(("dp", "expert"), None),
            P(("dp", "expert"), None),
            P(),
            P(("dp", "expert"), None),
            P(("dp", "expert"), None, None),
            P(("dp", "expert"), None, None),
        ),
        out_specs=P(("dp", "expert"), None),
        check_vma=False,
    )
```

```python
import functools

import jax
import jax.numpy as jnp
from jax import lax
from jax.experimental import pallas as pl
from jax.experimental.pallas import tpu as pltpu
from jax.sharding import PartitionSpec as P


def rms_norm(residual, norm_gain):
    scale_back = lax.rsqrt(jnp.mean(residual * residual, axis=-1, keepdims=True) + 1e-05)
    return (residual * scale_back * norm_gain).astype(jnp.bfloat16)


def route_block(expert_ids, split_pick, replica_expert):
    replica_total = replica_expert.shape[0]
    replica_iota = lax.iota(jnp.int32, replica_total)
    same_expert = replica_expert[:, None] == replica_expert[None, :]
    earlier = replica_iota[:, None] > replica_iota[None, :]
    replica_rank = jnp.sum((same_expert & earlier).astype(jnp.int32), axis=1)
    serves = expert_ids[:, :, None] == replica_expert[None, None, :]
    replica_count = jnp.sum(serves.astype(jnp.int32), axis=-1)
    wanted = split_pick % replica_count
    matches = serves & (replica_rank[None, None, :] == wanted[:, :, None])
    replica = jnp.sum(jnp.where(matches, replica_iota[None, None, :], 0), axis=-1)
    flat_replica = replica.reshape(-1)
    pair_iota = lax.iota(jnp.int32, flat_replica.shape[0])
    same_target = flat_replica[:, None] == flat_replica[None, :]
    before = pair_iota[:, None] > pair_iota[None, :]
    slot_index = jnp.sum((same_target & before).astype(jnp.int32), axis=1)
    return (replica, slot_index.reshape(replica.shape))


def apply_experts(incoming, up_gate, down, capacity):
    arrived_shape = incoming.shape
    local_reps = up_gate.shape[0]
    hidden_units = down.shape[1]
    stacked = incoming.reshape(-1, local_reps, capacity, incoming.shape[-1])
    gate_up = jnp.einsum("sjcd,jdf->sjcf", stacked, up_gate, preferred_element_type=jnp.float32)
    hidden_act = (jax.nn.silu(gate_up[..., :hidden_units]) * gate_up[..., hidden_units:]).astype(
        jnp.bfloat16
    )
    expert_out = jnp.einsum("sjcf,jfd->sjcd", hidden_act, down, preferred_element_type=jnp.float32)
    return expert_out.astype(jnp.bfloat16).reshape(arrived_shape)


def per_device(
    hidden_in,
    context,
    out_proj,
    norm_gain,
    router,
    expert_ids,
    replica_expert,
    split_pick,
    up_gate,
    down,
):
    tok_rows, model_width = hidden_in.shape
    top_count = expert_ids.shape[1]
    replica_total = replica_expert.shape[0]
    local_reps = up_gate.shape[0]
    data_groups = lax.axis_size("dp")
    expert_groups = lax.axis_size("expert")
    capacity = max(2, 2 * tok_rows * top_count // replica_total)
    summed = jnp.dot(
        context,
        lax.all_gather(out_proj, ("dp", "expert"), axis=0, tiled=True),
        preferred_element_type=jnp.float32,
    )
    router_rows = lax.all_gather(router, ("dp", "expert"), axis=0, tiled=True)
    residual = hidden_in.astype(jnp.float32) + summed
    normed = rms_norm(residual, norm_gain)
    logits = jnp.dot(normed, router_rows, preferred_element_type=jnp.float32)
    hit_mask = expert_ids[:, :, None] == lax.iota(jnp.int32, logits.shape[1])[None, None, :]
    chosen = jnp.sum(jnp.where(hit_mask, logits[:, None, :], 0.0), axis=-1)
    raised = jnp.exp(chosen)
    route_weight = raised / jnp.sum(raised, axis=-1, keepdims=True)
    replica, slot_index = route_block(expert_ids, split_pick, replica_expert)
    within_cap = slot_index < capacity
    buffer_row = jnp.where(within_cap, replica * capacity + slot_index, -1).reshape(-1)
    slot_total = replica_total * capacity
    matches = buffer_row[None, :] == lax.iota(jnp.int32, slot_total)[:, None]
    filled = jnp.any(matches, axis=1)
    row_of_pair = lax.iota(jnp.int32, tok_rows * top_count) // top_count
    anchor = jnp.sum(jnp.where(matches, row_of_pair[None, :], 0), axis=1)
    outgoing = jnp.where(filled[:, None], normed[anchor], jnp.zeros((), jnp.bfloat16))
    outgoing = outgoing.reshape(data_groups, expert_groups, local_reps * capacity, model_width)
    incoming = lax.all_to_all(
        lax.all_to_all(outgoing, "expert", split_axis=1, concat_axis=1, tiled=True),
        "dp",
        split_axis=0,
        concat_axis=0,
        tiled=True,
    )
    results = apply_experts(incoming, up_gate, down, capacity)
    returned = lax.all_to_all(
        lax.all_to_all(results, "dp", split_axis=0, concat_axis=0, tiled=True),
        "expert",
        split_axis=1,
        concat_axis=1,
        tiled=True,
    )
    returned = returned.reshape(slot_total, model_width)
    safe_index = jnp.where(within_cap, replica * capacity + slot_index, 0)
    gathered = returned[safe_index]
    kept_weight = jnp.where(within_cap, route_weight, 0.0)
    layer_out = residual + jnp.sum(kept_weight[:, :, None] * gathered.astype(jnp.float32), axis=1)
    return layer_out.astype(jnp.bfloat16)

MESH = pl.DeviceIdType.MESH
LINE = 4
SIDE = 128
CHUNKS = 4
FAR = LINE + 1
FIRST_LAG = 1
SECOND_LAG = 1
THIRD_LAG = 1
SIDE_LAG = 1
FIRST_LEAD = 0
SECOND_LEAD = 0
ROUTE_ROWS = 32
RING = 4
DOWN_RING = 2
GROUP = 4


def place():
    d, e = lax.axis_index("dp"), lax.axis_index("expert")
    return d // 2, d % 2, e // 2, e % 2


def device_of(y, c, z, x):
    return (y * 2 + c, z * 2 + x)


def block_of(y, c, z, x):
    return (y * 2 + c) * (2 * LINE) + z * 2 + x


def greet(barrier, y, c, z, x):
    for other in (device_of(y, 1 - c, z, x), device_of(1 - y, c, z, x), device_of(y, c, z, 1 - x)):
        pl.semaphore_signal(barrier, inc=1, device_id=other, device_id_type=MESH)

    @pl.when(z > 0)
    def _():
        pl.semaphore_signal(barrier, inc=1, device_id=device_of(y, c, z - 1, x), device_id_type=MESH)

    @pl.when(z < LINE - 1)
    def _():
        pl.semaphore_signal(barrier, inc=1, device_id=device_of(y, c, z + 1, x), device_id_type=MESH)

    pl.semaphore_wait(barrier, 3 + jnp.minimum(z, 1) + jnp.minimum(LINE - 1 - z, 1))


def plane_shift(q, p):
    qa, qb = q & 1, q >> 1
    return qb * (1 - p) + qa * p, qa * (1 - p) + qb * p


def chunk_kind(k):
    return k % 4 == 1, (3 * (k // 4) + (k % 4 + 1) // 2) % 2


def side_kind(k):
    return False, 1


def hops(q, far, m):
    return abs(far - m) + (q & 1) + (q >> 1)


class Place:
    def __init__(self):
        self.y, self.c, self.z, self.x = place()
        self.flip = self.z // 2
        self.m = self.z + self.flip * (LINE - 1 - 2 * self.z)
        self.outward = 1 - 2 * self.flip

    def z_of(self, far):
        return far + self.flip * (LINE - 1 - 2 * far)

    def plane(self, q, p):
        dy, dx = plane_shift(q, p)
        return (self.y + dy) % 2 if dy else self.y, (self.x + dx) % 2 if dx else self.x

    def seat(self, q, far, p):
        y, x = self.plane(q, p)
        return y * (2 * LINE) + self.z_of(far) * 2 + x

    def block(self, q, far, p):
        y, x = self.plane(q, p)
        return block_of(y, self.c, self.z_of(far), x)

    def over(self, q, p):
        y, x = self.plane(q, p)
        return device_of(y, self.c, self.z, x)

    def line(self, way):
        return device_of(self.y, self.c, self.z + way * self.outward, self.x)

    def twin(self):
        return device_of(self.y, 1 - self.c, self.z, self.x)

    def by_class(self, act):
        for m in range(2):
            @pl.when(self.m == m)
            def _(m=m):
                act(m)


def remote(src, dst, send_sem, recv_sem, target):
    return pltpu.make_async_remote_copy(
        src_ref=src, dst_ref=dst, send_sem=send_sem, recv_sem=recv_sem, device_id=target, device_id_type=MESH
    )


class Spread:
    def __init__(self, lag, lead, at, chunks, buf, blocks, kind, line_sem, twin_sem, recv_sem, twin_recv):
        self.at, self.chunks, self.buf, self.blocks, self.kind = at, chunks, buf, blocks, kind
        self.line_sem, self.twin_sem, self.recv_sem, self.twin_recv = line_sem, twin_sem, recv_sem, twin_recv
        self.sent = [0, 0]
        self.lag, self.lead = lag, lead

    def item(self, k, block):
        return self.buf.at[k * self.blocks + block]

    def event(self, k, q, far, m):
        at = self.at
        along_z, p = self.kind(k)
        item, recv = self.item(k, at.block(q, far, p)), self.recv_sem.at[k, at.seat(q, far, p)]
        targets = []
        if q == 0 or along_z:
            if far <= m:
                targets.append(at.line(1))
            if m > 0 and far >= m:
                targets.append(at.line(-1))
        if far == m or not along_z:
            if q <= 1:
                targets.append(at.over(2, p))
            if q == 0:
                targets.append(at.over(1, p))
        if q or far != m:
            remote(item, item, self.line_sem, recv, at.twin()).wait_recv()
        for target in targets:
            remote(item, item, self.line_sem, recv, target).start()
        self.sent[m] += len(targets)

    def twin(self, k, half, core):
        items = self.buf.at[pl.ds(k * self.blocks + (half * 2 + core) * 8, 8)]
        return remote(items, items, self.twin_sem, self.twin_recv.at[k, half], self.at.twin())

    def step(self, s, m):
        for reach in range(LINE + 2):
            for far in range(LINE):
                for q in range(4):
                    k = s - self.lag * reach + (self.lead if reach == 0 else 0)
                    if hops(q, far, m) != reach:
                        continue
                    if reach == 0 and s == 0:
                        for early in range(min(k, self.chunks)):
                            self.event(early, q, far, m)
                    if 0 <= k < self.chunks:
                        self.event(k, q, far, m)
        k = s - self.lag * (FAR - m)
        if 0 <= k < self.chunks:
            for half in range(2):
                self.twin(k, half, self.at.c).start()

    def ready(self, k):
        for half in range(2):
            self.twin(k, half, 1 - self.at.c).wait_recv()

    def drain(self):
        def act(m):
            items = self.buf.at[pl.ds(0, self.sent[m])]
            remote(items, items, self.line_sem, self.recv_sem.at[0, 0], self.at.twin()).wait_send()

        self.at.by_class(act)
        items = self.buf.at[pl.ds(0, self.chunks * 16)]
        remote(items, items, self.twin_sem, self.twin_recv.at[0, 0], self.at.twin()).wait_send()


def layer_kernel(
    plan, hid_ref, ctx_ref, proj_ref, gain_ref, router_ref, ids_ref, rep_ref, split_ref, up_ref, down_ref,
    out_ref, proj_buf, norm_buf, side_buf, weight_side, res_buf, up_ring, down_ring, acc_buf, act_buf, pick_buf,
    weight_buf, result_buf, core_buf, a_buf, b_buf, diag_buf, line_buf, line_end, scale_buf, local_sem, up_load,
    down_load, *sems
):
    tok_rows, width, top, capacity, reps, replica_total, expert_total, hidden_units, blocks = plan
    at = Place()
    y, c, z, x = at.y, at.c, at.z, at.x
    me = block_of(y, c, z, x)
    chunk = width // CHUNKS
    groups = blocks // GROUP
    group_rows = GROUP * tok_rows
    seats = GROUP * capacity
    slots = reps * seats
    unit = chunk
    units = width // unit
    f32, bf16 = jnp.float32, jnp.bfloat16

    def own_copy(k):
        return pltpu.make_async_copy(
            proj_ref.at[:, pl.ds(k * chunk, chunk)], proj_buf.at[k * blocks + me], local_sem.at[k]
        )

    def up_copy(i):
        u, j = i // reps, i % reps
        return pltpu.make_async_copy(
            up_ref.at[j, pl.ds(u * unit if isinstance(u, int) else pl.multiple_of(u * unit, unit), unit)], up_ring.at[i % RING], up_load.at[i % RING]
        )

    def down_copy(k):
        return pltpu.make_async_copy(
            down_ref.at[:, :, pl.ds(k * chunk, chunk)],
            down_ring.at[k % DOWN_RING],
            down_load.at[k % DOWN_RING],
        )

    for k in range(CHUNKS):
        own_copy(k).start()
    greet(pltpu.get_barrier_semaphore(), y, c, z, x)
    for i in range(RING):
        up_copy(i).start()
    for k in range(DOWN_RING):
        down_copy(k).start()

    first = Spread(FIRST_LAG, FIRST_LEAD, at, CHUNKS, proj_buf, blocks, chunk_kind, *sems[0:4])
    second = Spread(SECOND_LAG, SECOND_LEAD, at, CHUNKS, norm_buf, blocks, chunk_kind, *sems[4:8])
    first_side = Spread(FIRST_LAG, 0, at, 1, side_buf, blocks, side_kind, *sems[8:12])
    second_side = Spread(SIDE_LAG, 0, at, 1, weight_side, blocks, side_kind, *sems[12:16])
    twin_sem, twin_recv, hop_sem, a_recv, b_recv, diag_recv, line_recv, end_recv = sems[16:]

    for k in range(CHUNKS):
        own_copy(k).wait()
    at.by_class(lambda m: first.step(0, m))

    rep_row = jnp.broadcast_to(rep_ref[...], (replica_total, replica_total))
    row_i = lax.broadcasted_iota(jnp.int32, (replica_total, replica_total), 0)
    col_i = lax.broadcasted_iota(jnp.int32, (replica_total, replica_total), 1)
    rep_col = jnp.sum(jnp.where(row_i == col_i, rep_row, 0), axis=1, keepdims=True)
    rank = jnp.sum(jnp.where((rep_row == rep_col) & (col_i < row_i), 1, 0), axis=1, keepdims=True)
    replica_i = lax.broadcasted_iota(jnp.int32, (replica_total, tok_rows), 0)
    taken = jnp.zeros((replica_total, tok_rows), f32)
    hits, replicas = [], []
    for k in range(top):
        serves = rep_col == ids_ref[k : k + 1, :]
        count = jnp.sum(jnp.where(serves, 1.0, 0.0), axis=0, keepdims=True)
        pick = split_ref[k : k + 1, :].astype(f32)
        wanted = pick - jnp.floor((pick + 0.5) / count) * count
        hit = serves & (rank.astype(f32) == wanted)
        hits.append(hit)
        taken = jnp.where(hit, 1.0, taken)
        replicas.append(jnp.sum(jnp.where(hit, replica_i, 0).astype(f32), axis=0, keepdims=True))
    tok_i = lax.broadcasted_iota(jnp.int32, (tok_rows, tok_rows), 0)
    tok_j = lax.broadcasted_iota(jnp.int32, (tok_rows, tok_rows), 1)
    before = jnp.where(tok_i < tok_j, 1.0, 0.0).astype(bf16)
    earlier = jnp.dot(taken.astype(bf16), before, preferred_element_type=f32)
    slot_rows = [
        jnp.minimum(jnp.sum(jnp.where(hit, earlier, 0.0), axis=0, keepdims=True), float(capacity)) for hit in hits
    ]
    wide_i = lax.broadcasted_iota(jnp.int32, (tok_rows, SIDE), 0)
    wide_j = lax.broadcasted_iota(jnp.int32, (tok_rows, SIDE), 1)
    widen = jnp.where(wide_j == wide_i + x * tok_rows, 1.0, 0.0).astype(bf16)
    routing = jnp.concatenate(replicas + slot_rows, axis=0).astype(bf16)
    side_buf[me, ROUTE_ROWS:] = jnp.dot(routing, widen, preferred_element_type=f32).astype(bf16)
    half_i = lax.broadcasted_iota(jnp.int32, (expert_total, SIDE), 0)
    half_j = lax.broadcasted_iota(jnp.int32, (expert_total, SIDE), 1)
    packed = jnp.zeros((ROUTE_ROWS, SIDE), f32)
    for h in range(2):
        to_half = jnp.where(half_j == half_i + h * expert_total, 1.0, 0.0).astype(bf16)
        packed += jnp.dot(
            router_ref[h * ROUTE_ROWS : (h + 1) * ROUTE_ROWS, :], to_half, preferred_element_type=f32
        )
    side_buf[me, :ROUTE_ROWS] = packed.astype(bf16)

    def project(k):
        first.ready(k)
        weights = proj_buf[k * blocks : (k + 1) * blocks].reshape(width, chunk)
        summed = jnp.dot(ctx_ref[...], weights, preferred_element_type=f32)
        residual = hid_ref[:, k * chunk : (k + 1) * chunk].astype(f32) + summed
        res_buf[k] = residual
        norm_buf[k * blocks + me] = (residual * gain_ref[:, k * chunk : (k + 1) * chunk]).astype(bf16)

    def finish():
        square = jnp.zeros((tok_rows, 1), f32)
        for k in range(CHUNKS):
            square += jnp.sum(res_buf[k] * res_buf[k], axis=1, keepdims=True)
        scale_back = lax.rsqrt(square / width + 1e-05)
        low_logits = jnp.zeros((tok_rows, SIDE), f32)
        high_logits = low_logits
        share = chunk // tok_rows
        in_low = lax.broadcasted_iota(jnp.int32, (tok_rows, chunk), 1) % tok_rows < ROUTE_ROWS
        for k in range(CHUNKS):
            gain = gain_ref[:, k * chunk : (k + 1) * chunk]
            own = (res_buf[k] * scale_back * gain).astype(bf16).astype(f32)
            rows = side_buf[k * share : (k + 1) * share, :ROUTE_ROWS]
            rows = jnp.concatenate([rows, rows], axis=1).reshape(chunk, SIDE)
            low_logits += jnp.dot(jnp.where(in_low, own, 0.0).astype(bf16), rows, preferred_element_type=f32)
            high_logits += jnp.dot(jnp.where(in_low, 0.0, own).astype(bf16), rows, preferred_element_type=f32)
        logits = low_logits.T[:expert_total] + high_logits.T[expert_total:]
        expert_i = lax.broadcasted_iota(jnp.int32, (expert_total, tok_rows), 0)
        raised = [
            jnp.exp(jnp.sum(jnp.where(expert_i == ids_ref[k : k + 1, :], logits, 0.0), axis=0, keepdims=True))
            for k in range(top)
        ]
        raised = jnp.concatenate(raised, axis=0)
        route_weight = raised / jnp.sum(raised, axis=0, keepdims=True)
        upper = route_weight.astype(bf16).astype(f32)
        scale_row = jnp.broadcast_to(scale_back, (tok_rows, SIDE)).T[:1]
        scale_top = scale_row.astype(bf16).astype(f32)
        rest = jnp.zeros((2 * top - 2, tok_rows), f32)
        sent = jnp.concatenate([upper, route_weight - upper, scale_top, scale_row - scale_top, rest], axis=0).astype(bf16)
        weight_side[me] = jnp.dot(sent, widen, preferred_element_type=f32).astype(bf16)

    lane = lax.broadcasted_iota(jnp.int32, (1, group_rows), 1)
    slot_i = lax.broadcasted_iota(jnp.int32, (slots, group_rows), 0).astype(f32)
    seat_base = (lane // tok_rows * capacity).astype(f32)
    low = (me * reps).astype(f32)

    def group_side(ref, g, start, stop):
        def pair(i):
            return ref[GROUP * g + i, start:stop].astype(f32) + ref[GROUP * g + i + 1, start:stop].astype(f32)

        return jnp.concatenate([pair(0), pair(2)], axis=1)

    def seats_of(g):
        routed = group_side(side_buf, g, ROUTE_ROWS, ROUTE_ROWS + 2 * top)
        replica = routed[:top] - low
        slot = routed[top:]
        here = (replica >= 0) & (replica < reps) & (slot < capacity)
        return jnp.where(here, replica * seats + seat_base + slot, -1.0)

    def pick_body(g, carry):
        seat = seats_of(g)
        picked = jnp.zeros((slots, group_rows), f32)
        for k in range(top):
            picked = jnp.where(slot_i == seat[k : k + 1], 1.0, picked)
        pick_buf[g] = picked.astype(bf16)
        return carry

    def weigh_body(g, carry):
        seat = seats_of(g)
        weights = group_side(weight_side, g, 0, 2 * top)
        high = jnp.zeros((slots, group_rows), f32)
        rest = high
        for k in range(top):
            hit = slot_i == seat[k : k + 1]
            high = jnp.where(hit, weights[k : k + 1], high)
            rest = jnp.where(hit, weights[top + k : top + k + 1], rest)
        scales = group_side(weight_side, g, 2 * top, 2 * top + 2)
        scale = jnp.sum(pick_buf[g].astype(f32) * (scales[:1] + scales[1:]), axis=1, keepdims=True)
        for j in range(reps):
            scale_buf[j, pl.ds(pl.multiple_of(g * seats, seats), seats)] = jnp.broadcast_to(
                scale[j * seats : (j + 1) * seats], (seats, SIDE)
            )
        weight_buf[g, :, :slots] = high.T.astype(bf16)
        weight_buf[g, :, slots:] = rest.T.astype(bf16)
        return carry

    def take(k):
        second.ready(k)

        def body(g, carry):
            rows = norm_buf[pl.ds(k * blocks + g * GROUP, GROUP)].reshape(group_rows, chunk)
            taken = jnp.dot(pick_buf[g], rows, preferred_element_type=f32).astype(bf16)
            for j in range(reps):
                act_buf[
                    (k % 2) * reps + j,
                    pl.ds(pl.multiple_of(g * seats, seats), seats),
                ] = taken[j * seats : (j + 1) * seats]
            return carry

        lax.fori_loop(0, groups, body, 0)

    def raise_some(u, start, stop):
        def body(j, carry):
            i = u * reps + j
            up_copy(i).wait()
            expert_in = act_buf[(u % 2) * reps + j]
            for t in range(4):
                columns = slice(t * (2 * hidden_units // 4), (t + 1) * (2 * hidden_units // 4))
                acc_buf[j, :, columns] += jnp.dot(
                    expert_in, up_ring[i % RING, :, columns], preferred_element_type=f32
                )

            @pl.when(i + RING < units * reps)
            def _():
                up_copy(i + RING).start()

            return carry

        lax.fori_loop(start, stop, body, 0)

    acc_buf[...] = jnp.zeros_like(acc_buf)
    begin = FIRST_LAG * FAR + 1
    known = begin + CHUNKS
    used = begin + SECOND_LAG * FAR + 1
    side_end = known + SIDE_LAG * FAR + 1
    for s in range(1, max(used + CHUNKS, side_end + 1)):
        def gather_step(m, s=s):
            first.step(s, m)
            first_side.step(s - 1, m)
            second_side.step(s - known, m)

        at.by_class(gather_step)
        if begin <= s < begin + CHUNKS:
            project(s - begin)
        at.by_class(lambda m, s=s: second.step(s - begin, m))
        if s == begin + 1:
            first_side.ready(0)
            lax.fori_loop(0, groups, pick_body, 0)
        if s == known - 1:
            finish()
        if used <= s < used + CHUNKS:
            take(s - used)
            raise_some(s - used, 0, reps)
        if s == side_end:
            second_side.ready(0)
            lax.fori_loop(0, groups, weigh_body, 0)

    def act_body(j, carry):
        scale = scale_buf[j, :, :1]
        for h in range(2):
            half = hidden_units // 2
            gate = acc_buf[j, :, h * half : (h + 1) * half] * scale
            raised = acc_buf[j, :, hidden_units + h * half : hidden_units + (h + 1) * half] * scale
            act_buf[2 * j + h] = (gate / (1.0 + jnp.exp(-gate)) * raised).astype(bf16)
        return carry

    lax.fori_loop(0, reps, act_body, 0)
    first.drain()
    first_side.drain()

    def lower_chunk(k):
        down_copy(k).wait()
        for j in range(reps):
            half = hidden_units // 2
            result = jnp.dot(act_buf[2 * j], down_ring[k % DOWN_RING, j, :half], preferred_element_type=f32)
            result += jnp.dot(act_buf[2 * j + 1], down_ring[k % DOWN_RING, j, half:], preferred_element_type=f32)
            result = result.astype(bf16)
            for g in range(groups):
                some = result[g * seats : (g + 1) * seats]
                result_buf[g, j * seats : (j + 1) * seats] = some
                result_buf[g, slots + j * seats : slots + (j + 1) * seats] = some

        if k + DOWN_RING < CHUNKS:
            down_copy(k + DOWN_RING).start()

        def body(g, carry):
            summed = jnp.dot(weight_buf[g], result_buf[g], preferred_element_type=f32).astype(bf16)
            proj_buf[pl.ds(k * blocks + g * GROUP, GROUP)] = summed.reshape(GROUP, tok_rows, chunk)
            return carry

        lax.fori_loop(0, groups, body, 0)

    def to_twin(k, half):
        return remote(
            proj_buf.at[pl.ds(k * blocks + (half * 2 + 1 - c) * 8, 8)],
            core_buf.at[pl.ds(k * 16 + half * 8, 8)],
            twin_sem,
            twin_recv.at[k, half],
            at.twin(),
        )

    def line_slot(k, q, far):
        before = sum(4 * LINE if chunk_kind(i)[0] else LINE for i in range(k))
        return before + q * LINE + at.z_of(far)

    def end_slot(k, q):
        return sum(4 if chunk_kind(i)[0] else 1 for i in range(k)) + q

    hop_count = [0, 0]

    def join(k, q, far, m):
        along_z, p = chunk_kind(k)
        target_z = at.z_of(far)
        in_plane = far == m or not along_z
        children = []
        if q == 1 and in_plane:
            children.append((diag_buf.at[k * LINE + target_z], diag_recv.at[k, target_z]))
        if q == 0 and in_plane:
            children.append((a_buf.at[k * LINE + target_z], a_recv.at[k, target_z]))
            children.append((b_buf.at[k * LINE + target_z], b_recv.at[k, target_z]))
        if q == 0 or along_z:
            if far <= m or m > 0:
                slot = line_slot(k, q, far)
                children.append((line_buf.at[slot], line_recv.at[slot]))
            if far == m and m > 0:
                slot = end_slot(k, q)
                children.append((line_end.at[slot], end_recv.at[slot]))
        held = core_buf.at[k * 16 + at.seat(q, far, p)]
        for ref, sem in children:
            remote(ref, ref, hop_sem, sem, at.twin()).wait_recv()
        total = held[...].astype(f32) + proj_buf[k * blocks + at.block(q, far, p)].astype(f32)
        for ref, _ in children:
            total += ref[...].astype(f32)
        if q == 0 and far == m:
            out_ref[:, k * chunk : (k + 1) * chunk] = (res_buf[k] + total).astype(bf16)
            return
        held[...] = total.astype(bf16)
        if q and in_plane:
            buf, sem = {1: (a_buf, a_recv), 2: (b_buf, b_recv), 3: (diag_buf, diag_recv)}[q]
            dst, recv = buf.at[k * LINE + target_z], sem.at[k, target_z]
            target = at.over(1 if q == 1 else 2, p)
        else:
            target = at.line(1 if far > m else -1)
            if m == 0 and far == 1:
                slot = end_slot(k, q)
                dst, recv = line_end.at[slot], end_recv.at[slot]
            else:
                slot = line_slot(k, q, far)
                dst, recv = line_buf.at[slot], line_recv.at[slot]
        remote(held, dst, hop_sem, recv, target).start()
        hop_count[m] += 1

    def join_step(s, m):
        for reach in range(LINE + 1, -1, -1):
            for q in (3, 1, 2, 0):
                for far in range(LINE - 1, -1, -1):
                    k = s - 1 - THIRD_LAG * (FAR - reach)
                    if hops(q, far, m) == reach and 0 <= k < CHUNKS:
                        join(k, q, far, m)

    for s in range(CHUNKS + THIRD_LAG * FAR + 1):
        if 1 <= s <= CHUNKS:
            for half in range(2):
                to_twin(s - 1, half).wait_recv()
        at.by_class(lambda m: join_step(s, m))
        if s < CHUNKS:
            lower_chunk(s)
            for half in range(2):
                to_twin(s, half).start()

    def hop_drain(m):
        items = core_buf.at[pl.ds(0, hop_count[m])]
        remote(items, items, hop_sem, a_recv.at[0, 0], at.twin()).wait_send()

    at.by_class(hop_drain)
    items = core_buf.at[pl.ds(0, CHUNKS * 16)]
    remote(items, items, twin_sem, twin_recv.at[0, 0], at.twin()).wait_send()
    second.drain()
    second_side.drain()


def run_layer(
    hidden_in, context, out_proj, norm_gain, router, expert_ids, replica_expert, split_pick, up_gate, down
):
    tok_rows, width = hidden_in.shape
    top = expert_ids.shape[1]
    replica_total = replica_expert.shape[0]
    expert_total = router.shape[1]
    reps, hidden_units, _ = down.shape
    blocks = lax.axis_size("dp") * lax.axis_size("expert")
    capacity = max(2, 2 * tok_rows * top // replica_total)
    chunk = width // CHUNKS
    groups = blocks // GROUP
    seats = GROUP * capacity
    slots = reps * seats
    dma = pltpu.SemaphoreType.DMA
    vmem, anywhere = pl.BlockSpec(memory_space=pltpu.VMEM), pl.BlockSpec(memory_space=pl.ANY)

    def spread_sems(chunks):
        return [dma, dma, dma((chunks, 16)), dma((chunks, 2))]

    lines = sum(4 if chunk_kind(k)[0] else 1 for k in range(CHUNKS))
    bf16, f32 = jnp.bfloat16, jnp.float32
    plan = (tok_rows, width, top, capacity, reps, replica_total, expert_total, hidden_units, blocks)
    return pl.pallas_call(
        functools.partial(layer_kernel, plan),
        out_shape=jax.ShapeDtypeStruct((tok_rows, width), bf16),
        in_specs=[vmem, vmem, anywhere, vmem, vmem, vmem, vmem, vmem, anywhere, anywhere],
        out_specs=vmem,
        scratch_shapes=[
            pltpu.VMEM((CHUNKS * blocks, tok_rows, chunk), bf16),
            pltpu.VMEM((CHUNKS * blocks, tok_rows, chunk), bf16),
            pltpu.VMEM((blocks, ROUTE_ROWS + 2 * top, SIDE), bf16),
            pltpu.VMEM((blocks, 4 * top, SIDE), bf16),
            pltpu.VMEM((CHUNKS, tok_rows, chunk), f32),
            pltpu.VMEM((RING, chunk, 2 * hidden_units), bf16),
            pltpu.VMEM((DOWN_RING, reps, hidden_units, chunk), bf16),
            pltpu.VMEM((reps, groups * seats, 2 * hidden_units), f32),
            pltpu.VMEM((2 * reps, groups * seats, hidden_units // 2), bf16),
            pltpu.VMEM((groups, slots, GROUP * tok_rows), bf16),
            pltpu.VMEM((groups, GROUP * tok_rows, 2 * slots), bf16),
            pltpu.VMEM((groups, 2 * slots, chunk), bf16),
            pltpu.VMEM((CHUNKS * 16, tok_rows, chunk), bf16),
            pltpu.VMEM((CHUNKS * LINE, tok_rows, chunk), bf16),
            pltpu.VMEM((CHUNKS * LINE, tok_rows, chunk), bf16),
            pltpu.VMEM((CHUNKS * LINE, tok_rows, chunk), bf16),
            pltpu.VMEM((lines * LINE, tok_rows, chunk), bf16),
            pltpu.VMEM((lines, tok_rows, chunk), bf16),
            pltpu.VMEM((reps, groups * seats, SIDE), f32),
            dma((CHUNKS,)),
            dma((RING,)),
            dma((DOWN_RING,)),
        ]
        + spread_sems(CHUNKS)
        + spread_sems(CHUNKS)
        + spread_sems(1)
        + spread_sems(1)
        + [
            dma,
            dma((CHUNKS, 2)),
            dma,
            dma((CHUNKS, LINE)),
            dma((CHUNKS, LINE)),
            dma((CHUNKS, LINE)),
            dma((lines * LINE,)),
            dma((lines,)),
        ],
        compiler_params=pltpu.CompilerParams(collective_id=0, has_side_effects=True, vmem_limit_bytes=62 << 20),
    )(
        hidden_in, context, out_proj, norm_gain.reshape(1, width), router, expert_ids.T,
        replica_expert.reshape(1, replica_total), split_pick.T, up_gate, down,
    )


def solution(mesh):
    plan = run_layer if (mesh.shape["dp"], mesh.shape["expert"]) == (4, 8) else per_device
    return jax.shard_map(
        plan,
        mesh=mesh,
        in_specs=(
            P(("dp", "expert"), None),
            P(("dp", "expert"), None),
            P(("dp", "expert"), None),
            P(),
            P(("dp", "expert"), None),
            P(("dp", "expert"), None),
            P(),
            P(("dp", "expert"), None),
            P(("dp", "expert"), None, None),
            P(("dp", "expert"), None, None),
        ),
        out_specs=P(("dp", "expert"), None),
        check_vma=False,
    )
```

```python
import functools

import jax
import jax.numpy as jnp
from jax import lax
from jax.experimental import pallas as pl
from jax.experimental.pallas import tpu as pltpu
from jax.sharding import PartitionSpec as P


def rms_norm(residual, norm_gain):
    scale_back = lax.rsqrt(jnp.mean(residual * residual, axis=-1, keepdims=True) + 1e-05)
    return (residual * scale_back * norm_gain).astype(jnp.bfloat16)


def route_block(expert_ids, split_pick, replica_expert):
    replica_total = replica_expert.shape[0]
    replica_iota = lax.iota(jnp.int32, replica_total)
    same_expert = replica_expert[:, None] == replica_expert[None, :]
    earlier = replica_iota[:, None] > replica_iota[None, :]
    replica_rank = jnp.sum((same_expert & earlier).astype(jnp.int32), axis=1)
    serves = expert_ids[:, :, None] == replica_expert[None, None, :]
    replica_count = jnp.sum(serves.astype(jnp.int32), axis=-1)
    wanted = split_pick % replica_count
    matches = serves & (replica_rank[None, None, :] == wanted[:, :, None])
    replica = jnp.sum(jnp.where(matches, replica_iota[None, None, :], 0), axis=-1)
    flat_replica = replica.reshape(-1)
    pair_iota = lax.iota(jnp.int32, flat_replica.shape[0])
    same_target = flat_replica[:, None] == flat_replica[None, :]
    before = pair_iota[:, None] > pair_iota[None, :]
    slot_index = jnp.sum((same_target & before).astype(jnp.int32), axis=1)
    return (replica, slot_index.reshape(replica.shape))


def apply_experts(incoming, up_gate, down, capacity):
    arrived_shape = incoming.shape
    local_reps = up_gate.shape[0]
    hidden_units = down.shape[1]
    stacked = incoming.reshape(-1, local_reps, capacity, incoming.shape[-1])
    gate_up = jnp.einsum("sjcd,jdf->sjcf", stacked, up_gate, preferred_element_type=jnp.float32)
    hidden_act = (jax.nn.silu(gate_up[..., :hidden_units]) * gate_up[..., hidden_units:]).astype(
        jnp.bfloat16
    )
    expert_out = jnp.einsum("sjcf,jfd->sjcd", hidden_act, down, preferred_element_type=jnp.float32)
    return expert_out.astype(jnp.bfloat16).reshape(arrived_shape)


def per_device(
    hidden_in,
    context,
    out_proj,
    norm_gain,
    router,
    expert_ids,
    replica_expert,
    split_pick,
    up_gate,
    down,
):
    tok_rows, model_width = hidden_in.shape
    top_count = expert_ids.shape[1]
    replica_total = replica_expert.shape[0]
    local_reps = up_gate.shape[0]
    data_groups = lax.axis_size("dp")
    expert_groups = lax.axis_size("expert")
    capacity = max(2, 2 * tok_rows * top_count // replica_total)
    summed = jnp.dot(
        context,
        lax.all_gather(out_proj, ("dp", "expert"), axis=0, tiled=True),
        preferred_element_type=jnp.float32,
    )
    router_rows = lax.all_gather(router, ("dp", "expert"), axis=0, tiled=True)
    residual = hidden_in.astype(jnp.float32) + summed
    normed = rms_norm(residual, norm_gain)
    logits = jnp.dot(normed, router_rows, preferred_element_type=jnp.float32)
    hit_mask = expert_ids[:, :, None] == lax.iota(jnp.int32, logits.shape[1])[None, None, :]
    chosen = jnp.sum(jnp.where(hit_mask, logits[:, None, :], 0.0), axis=-1)
    raised = jnp.exp(chosen)
    route_weight = raised / jnp.sum(raised, axis=-1, keepdims=True)
    replica, slot_index = route_block(expert_ids, split_pick, replica_expert)
    within_cap = slot_index < capacity
    buffer_row = jnp.where(within_cap, replica * capacity + slot_index, -1).reshape(-1)
    slot_total = replica_total * capacity
    matches = buffer_row[None, :] == lax.iota(jnp.int32, slot_total)[:, None]
    filled = jnp.any(matches, axis=1)
    row_of_pair = lax.iota(jnp.int32, tok_rows * top_count) // top_count
    anchor = jnp.sum(jnp.where(matches, row_of_pair[None, :], 0), axis=1)
    outgoing = jnp.where(filled[:, None], normed[anchor], jnp.zeros((), jnp.bfloat16))
    outgoing = outgoing.reshape(data_groups, expert_groups, local_reps * capacity, model_width)
    incoming = lax.all_to_all(
        lax.all_to_all(outgoing, "expert", split_axis=1, concat_axis=1, tiled=True),
        "dp",
        split_axis=0,
        concat_axis=0,
        tiled=True,
    )
    results = apply_experts(incoming, up_gate, down, capacity)
    returned = lax.all_to_all(
        lax.all_to_all(results, "dp", split_axis=0, concat_axis=0, tiled=True),
        "expert",
        split_axis=1,
        concat_axis=1,
        tiled=True,
    )
    returned = returned.reshape(slot_total, model_width)
    safe_index = jnp.where(within_cap, replica * capacity + slot_index, 0)
    gathered = returned[safe_index]
    kept_weight = jnp.where(within_cap, route_weight, 0.0)
    layer_out = residual + jnp.sum(kept_weight[:, :, None] * gathered.astype(jnp.float32), axis=1)
    return layer_out.astype(jnp.bfloat16)

MESH = pl.DeviceIdType.MESH
LINE = 4
SIDE = 128
CHUNKS = 4
FAR = LINE + 1
FIRST_LAG = 1
SECOND_LAG = 1
THIRD_LAG = 1
SIDE_LAG = 1
FIRST_LEAD = 0
SECOND_LEAD = 0
ROUTE_ROWS = 32
RING = 4
DOWN_RING = 2
GROUP = 4


def place():
    d, e = lax.axis_index("dp"), lax.axis_index("expert")
    return d // 2, d % 2, e // 2, e % 2


def device_of(y, c, z, x):
    return (y * 2 + c, z * 2 + x)


def block_of(y, c, z, x):
    return (y * 2 + c) * (2 * LINE) + z * 2 + x


def greet(barrier, y, c, z, x):
    for other in (device_of(y, 1 - c, z, x), device_of(1 - y, c, z, x), device_of(y, c, z, 1 - x)):
        pl.semaphore_signal(barrier, inc=1, device_id=other, device_id_type=MESH)

    @pl.when(z > 0)
    def _():
        pl.semaphore_signal(barrier, inc=1, device_id=device_of(y, c, z - 1, x), device_id_type=MESH)

    @pl.when(z < LINE - 1)
    def _():
        pl.semaphore_signal(barrier, inc=1, device_id=device_of(y, c, z + 1, x), device_id_type=MESH)

    pl.semaphore_wait(barrier, 3 + jnp.minimum(z, 1) + jnp.minimum(LINE - 1 - z, 1))


def plane_shift(q, p):
    qa, qb = q & 1, q >> 1
    return qb * (1 - p) + qa * p, qa * (1 - p) + qb * p


def chunk_kind(k):
    return k % 4 == 1, (3 * (k // 4) + (k % 4 + 1) // 2) % 2


def side_kind(k):
    return False, 1


def hops(q, far, m):
    return abs(far - m) + (q & 1) + (q >> 1)


class Place:
    def __init__(self):
        self.y, self.c, self.z, self.x = place()
        self.flip = self.z // 2
        self.m = self.z + self.flip * (LINE - 1 - 2 * self.z)
        self.outward = 1 - 2 * self.flip

    def z_of(self, far):
        return far + self.flip * (LINE - 1 - 2 * far)

    def plane(self, q, p):
        dy, dx = plane_shift(q, p)
        return (self.y + dy) % 2 if dy else self.y, (self.x + dx) % 2 if dx else self.x

    def seat(self, q, far, p):
        y, x = self.plane(q, p)
        return y * (2 * LINE) + self.z_of(far) * 2 + x

    def block(self, q, far, p):
        y, x = self.plane(q, p)
        return block_of(y, self.c, self.z_of(far), x)

    def over(self, q, p):
        y, x = self.plane(q, p)
        return device_of(y, self.c, self.z, x)

    def line(self, way):
        return device_of(self.y, self.c, self.z + way * self.outward, self.x)

    def twin(self):
        return device_of(self.y, 1 - self.c, self.z, self.x)

    def by_class(self, act):
        for m in range(2):
            @pl.when(self.m == m)
            def _(m=m):
                act(m)


def remote(src, dst, send_sem, recv_sem, target):
    return pltpu.make_async_remote_copy(
        src_ref=src, dst_ref=dst, send_sem=send_sem, recv_sem=recv_sem, device_id=target, device_id_type=MESH
    )


class Spread:
    def __init__(self, lag, lead, at, chunks, buf, blocks, kind, line_sem, twin_sem, recv_sem, twin_recv):
        self.at, self.chunks, self.buf, self.blocks, self.kind = at, chunks, buf, blocks, kind
        self.line_sem, self.twin_sem, self.recv_sem, self.twin_recv = line_sem, twin_sem, recv_sem, twin_recv
        self.sent = [0, 0]
        self.lag, self.lead = lag, lead

    def item(self, k, block):
        return self.buf.at[k * self.blocks + block]

    def event(self, k, q, far, m):
        at = self.at
        along_z, p = self.kind(k)
        item, recv = self.item(k, at.block(q, far, p)), self.recv_sem.at[k, at.seat(q, far, p)]
        targets = []
        if q == 0 or along_z:
            if far <= m:
                targets.append(at.line(1))
            if m > 0 and far >= m:
                targets.append(at.line(-1))
        if far == m or not along_z:
            if q <= 1:
                targets.append(at.over(2, p))
            if q == 0:
                targets.append(at.over(1, p))
        if q or far != m:
            remote(item, item, self.line_sem, recv, at.twin()).wait_recv()
        for target in targets:
            remote(item, item, self.line_sem, recv, target).start()
        self.sent[m] += len(targets)

    def twin(self, k, half, core):
        items = self.buf.at[pl.ds(k * self.blocks + (half * 2 + core) * 8, 8)]
        return remote(items, items, self.twin_sem, self.twin_recv.at[k, half], self.at.twin())

    def step(self, s, m):
        for reach in range(LINE + 2):
            for far in range(LINE):
                for q in range(4):
                    k = s - self.lag * reach + (self.lead if reach == 0 else 0)
                    if hops(q, far, m) != reach:
                        continue
                    if reach == 0 and s == 0:
                        for early in range(min(k, self.chunks)):
                            self.event(early, q, far, m)
                    if 0 <= k < self.chunks:
                        self.event(k, q, far, m)
        k = s - self.lag * (FAR - m)
        if 0 <= k < self.chunks:
            for half in range(2):
                self.twin(k, half, self.at.c).start()

    def ready(self, k):
        for half in range(2):
            self.twin(k, half, 1 - self.at.c).wait_recv()

    def drain(self):
        def act(m):
            items = self.buf.at[pl.ds(0, self.sent[m])]
            remote(items, items, self.line_sem, self.recv_sem.at[0, 0], self.at.twin()).wait_send()

        self.at.by_class(act)
        items = self.buf.at[pl.ds(0, self.chunks * 16)]
        remote(items, items, self.twin_sem, self.twin_recv.at[0, 0], self.at.twin()).wait_send()


def layer_kernel(
    plan, hid_ref, ctx_ref, proj_ref, gain_ref, router_ref, ids_ref, rep_ref, split_ref, up_ref, down_ref,
    out_ref, proj_buf, norm_buf, side_buf, weight_side, res_buf, up_ring, down_ring, acc_buf, act_buf, pick_buf,
    place_buf, weight_buf, result_buf, core_buf, a_buf, b_buf, diag_buf, line_buf, line_end, scale_buf, local_sem, up_load,
    down_load, *sems
):
    tok_rows, width, top, capacity, reps, replica_total, expert_total, hidden_units, blocks = plan
    at = Place()
    y, c, z, x = at.y, at.c, at.z, at.x
    me = block_of(y, c, z, x)
    chunk = width // CHUNKS
    groups = blocks // GROUP
    group_rows = GROUP * tok_rows
    seats = GROUP * capacity
    slots = reps * seats
    parts = hidden_units // 2 // chunk
    unit = parts * chunk
    units = width // unit
    f32, bf16 = jnp.float32, jnp.bfloat16

    def own_copy(k):
        return pltpu.make_async_copy(
            proj_ref.at[:, pl.ds(k * chunk, chunk)], proj_buf.at[k * blocks + me], local_sem.at[k]
        )

    def up_copy(i):
        u, j = i // reps, i % reps
        return pltpu.make_async_copy(
            up_ref.at[j, pl.ds(u * unit if isinstance(u, int) else pl.multiple_of(u * unit, unit), unit)], up_ring.at[i % RING], up_load.at[i % RING]
        )

    def down_copy(k):
        return pltpu.make_async_copy(
            down_ref.at[:, :, pl.ds(k * chunk, chunk)],
            down_ring.at[k % DOWN_RING],
            down_load.at[k % DOWN_RING],
        )

    for k in range(CHUNKS):
        own_copy(k).start()
    greet(pltpu.get_barrier_semaphore(), y, c, z, x)
    for i in range(RING):
        up_copy(i).start()
    for k in range(DOWN_RING):
        down_copy(k).start()

    first = Spread(FIRST_LAG, FIRST_LEAD, at, CHUNKS, proj_buf, blocks, chunk_kind, *sems[0:4])
    second = Spread(SECOND_LAG, SECOND_LEAD, at, CHUNKS, norm_buf, blocks, chunk_kind, *sems[4:8])
    first_side = Spread(FIRST_LAG, 0, at, 1, side_buf, blocks, side_kind, *sems[8:12])
    second_side = Spread(SIDE_LAG, 0, at, 1, weight_side, blocks, side_kind, *sems[12:16])
    twin_sem, twin_recv, hop_sem, a_recv, b_recv, diag_recv, line_recv, end_recv = sems[16:]

    for k in range(CHUNKS):
        own_copy(k).wait()
    at.by_class(lambda m: first.step(0, m))

    rep_row = jnp.broadcast_to(rep_ref[...], (replica_total, replica_total))
    row_i = lax.broadcasted_iota(jnp.int32, (replica_total, replica_total), 0)
    col_i = lax.broadcasted_iota(jnp.int32, (replica_total, replica_total), 1)
    rep_col = jnp.sum(jnp.where(row_i == col_i, rep_row, 0), axis=1, keepdims=True)
    rank = jnp.sum(jnp.where((rep_row == rep_col) & (col_i < row_i), 1, 0), axis=1, keepdims=True)
    replica_i = lax.broadcasted_iota(jnp.int32, (replica_total, tok_rows), 0)
    taken = jnp.zeros((replica_total, tok_rows), f32)
    hits, replicas = [], []
    for k in range(top):
        serves = rep_col == ids_ref[k : k + 1, :]
        count = jnp.sum(jnp.where(serves, 1.0, 0.0), axis=0, keepdims=True)
        pick = split_ref[k : k + 1, :].astype(f32)
        wanted = pick - jnp.floor((pick + 0.5) / count) * count
        hit = serves & (rank.astype(f32) == wanted)
        hits.append(hit)
        taken = jnp.where(hit, 1.0, taken)
        replicas.append(jnp.sum(jnp.where(hit, replica_i, 0).astype(f32), axis=0, keepdims=True))
    tok_i = lax.broadcasted_iota(jnp.int32, (tok_rows, tok_rows), 0)
    tok_j = lax.broadcasted_iota(jnp.int32, (tok_rows, tok_rows), 1)
    before = jnp.where(tok_i < tok_j, 1.0, 0.0).astype(bf16)
    earlier = jnp.dot(taken.astype(bf16), before, preferred_element_type=f32)
    slot_rows = [
        jnp.minimum(jnp.sum(jnp.where(hit, earlier, 0.0), axis=0, keepdims=True), float(capacity)) for hit in hits
    ]
    wide_i = lax.broadcasted_iota(jnp.int32, (tok_rows, SIDE), 0)
    wide_j = lax.broadcasted_iota(jnp.int32, (tok_rows, SIDE), 1)
    widen = jnp.where(wide_j == wide_i + x * tok_rows, 1.0, 0.0).astype(bf16)
    routing = jnp.concatenate(replicas + slot_rows, axis=0).astype(bf16)
    side_buf[me, ROUTE_ROWS:] = jnp.dot(routing, widen, preferred_element_type=f32).astype(bf16)
    half_i = lax.broadcasted_iota(jnp.int32, (expert_total, SIDE), 0)
    half_j = lax.broadcasted_iota(jnp.int32, (expert_total, SIDE), 1)
    packed = jnp.zeros((ROUTE_ROWS, SIDE), f32)
    for h in range(2):
        to_half = jnp.where(half_j == half_i + h * expert_total, 1.0, 0.0).astype(bf16)
        packed += jnp.dot(
            router_ref[h * ROUTE_ROWS : (h + 1) * ROUTE_ROWS, :], to_half, preferred_element_type=f32
        )
    side_buf[me, :ROUTE_ROWS] = packed.astype(bf16)

    def project(k):
        first.ready(k)
        weights = proj_buf[k * blocks : (k + 1) * blocks].reshape(width, chunk)
        summed = jnp.dot(ctx_ref[...], weights, preferred_element_type=f32)
        residual = hid_ref[:, k * chunk : (k + 1) * chunk].astype(f32) + summed
        res_buf[k] = residual
        norm_buf[k * blocks + me] = (residual * gain_ref[:, k * chunk : (k + 1) * chunk]).astype(bf16)

    def finish():
        square = jnp.zeros((tok_rows, 1), f32)
        for k in range(CHUNKS):
            square += jnp.sum(res_buf[k] * res_buf[k], axis=1, keepdims=True)
        scale_back = lax.rsqrt(square / width + 1e-05)
        low_logits = jnp.zeros((tok_rows, SIDE), f32)
        high_logits = low_logits
        share = chunk // tok_rows
        in_low = lax.broadcasted_iota(jnp.int32, (tok_rows, chunk), 1) % tok_rows < ROUTE_ROWS
        for k in range(CHUNKS):
            gain = gain_ref[:, k * chunk : (k + 1) * chunk]
            own = (res_buf[k] * scale_back * gain).astype(bf16).astype(f32)
            rows = side_buf[k * share : (k + 1) * share, :ROUTE_ROWS]
            rows = jnp.concatenate([rows, rows], axis=1).reshape(chunk, SIDE)
            low_logits += jnp.dot(jnp.where(in_low, own, 0.0).astype(bf16), rows, preferred_element_type=f32)
            high_logits += jnp.dot(jnp.where(in_low, 0.0, own).astype(bf16), rows, preferred_element_type=f32)
        logits = low_logits.T[:expert_total] + high_logits.T[expert_total:]
        expert_i = lax.broadcasted_iota(jnp.int32, (expert_total, tok_rows), 0)
        raised = [
            jnp.exp(jnp.sum(jnp.where(expert_i == ids_ref[k : k + 1, :], logits, 0.0), axis=0, keepdims=True))
            for k in range(top)
        ]
        raised = jnp.concatenate(raised, axis=0)
        route_weight = raised / jnp.sum(raised, axis=0, keepdims=True)
        upper = route_weight.astype(bf16).astype(f32)
        scale_row = jnp.broadcast_to(scale_back, (tok_rows, SIDE)).T[:1]
        scale_top = scale_row.astype(bf16).astype(f32)
        rest = jnp.zeros((2 * top - 2, tok_rows), f32)
        sent = jnp.concatenate([upper, route_weight - upper, scale_top, scale_row - scale_top, rest], axis=0).astype(bf16)
        weight_side[me] = jnp.dot(sent, widen, preferred_element_type=f32).astype(bf16)

    lane = lax.broadcasted_iota(jnp.int32, (1, group_rows), 1)
    slot_i = lax.broadcasted_iota(jnp.int32, (slots, group_rows), 0).astype(f32)
    seat_base = (lane // tok_rows * capacity).astype(f32)
    low = (me * reps).astype(f32)

    def group_side(ref, g, start, stop):
        def pair(i):
            return ref[GROUP * g + i, start:stop].astype(f32) + ref[GROUP * g + i + 1, start:stop].astype(f32)

        return jnp.concatenate([pair(0), pair(2)], axis=1)

    def seats_of(g):
        routed = group_side(side_buf, g, ROUTE_ROWS, ROUTE_ROWS + 2 * top)
        replica = routed[:top] - low
        slot = routed[top:]
        here = (replica >= 0) & (replica < reps) & (slot < capacity)
        return jnp.where(here, replica * seats + seat_base + slot, -1.0)

    def pick_body(g, carry):
        seat = seats_of(g)
        picked = jnp.zeros((slots, group_rows), f32)
        for k in range(top):
            picked = jnp.where(slot_i == seat[k : k + 1], 1.0, picked)
        pick_buf[g] = picked.astype(bf16)
        place_buf[g] = picked.T.astype(bf16)
        return carry

    def weigh_body(g, carry):
        seat = seats_of(g)
        weights = group_side(weight_side, g, 0, 2 * top)
        weights = weights[:top] + weights[top:]
        weighed = jnp.zeros((slots, group_rows), f32)
        for k in range(top):
            weighed = jnp.where(slot_i == seat[k : k + 1], weights[k : k + 1], weighed)
        weight = jnp.sum(weighed, axis=1, keepdims=True)
        scales = group_side(weight_side, g, 2 * top, 2 * top + 2)
        scale = jnp.sum(pick_buf[g].astype(f32) * (scales[:1] + scales[1:]), axis=1, keepdims=True)
        for j in range(reps):
            rows = pl.ds(pl.multiple_of(g * seats, seats), seats)
            scale_buf[j, rows] = jnp.broadcast_to(scale[j * seats : (j + 1) * seats], (seats, SIDE))
            weight_buf[j, rows] = jnp.broadcast_to(weight[j * seats : (j + 1) * seats], (seats, SIDE))
        return carry

    def take(k):
        second.ready(k)

        def body(g, carry):
            rows = norm_buf[pl.ds(k * blocks + g * GROUP, GROUP)].reshape(group_rows, chunk)
            taken = jnp.dot(pick_buf[g], rows, preferred_element_type=f32).astype(bf16)
            for j in range(reps):
                act_buf[
                    (k // parts % 2) * reps + j,
                    pl.ds(pl.multiple_of(g * seats, seats), seats),
                    (k % parts) * chunk : (k % parts + 1) * chunk,
                ] = taken[j * seats : (j + 1) * seats]
            return carry

        lax.fori_loop(0, groups, body, 0)

    def activate(j):
        scale = scale_buf[j, :, :1]
        for h in range(2):
            half = hidden_units // 2
            gate = acc_buf[j, :, h * half : (h + 1) * half] * scale
            raised = acc_buf[j, :, hidden_units + h * half : hidden_units + (h + 1) * half] * scale
            act_buf[2 * j + h] = (gate / (1.0 + jnp.exp(-gate)) * raised).astype(bf16)

    def raise_some(u, start, stop):
        depth = slice(start * chunk, stop * chunk)

        last = u == units - 1 and stop == parts

        def body(j, carry):
            i = u * reps + j
            if last and j:
                activate(j - 1)
            if start == 0:
                up_copy(i).wait()
            expert_in = act_buf[(u % 2) * reps + j, :, depth]
            for t in range(4):
                columns = slice(t * (2 * hidden_units // 4), (t + 1) * (2 * hidden_units // 4))
                acc_buf[j, :, columns] += jnp.dot(
                    expert_in, up_ring[i % RING, depth, columns], preferred_element_type=f32
                )
            if stop == parts and u < units - 1:
                up_copy(i + RING).start()
            return carry

        if last:
            for j in range(reps):
                body(j, 0)
            activate(reps - 1)
        else:
            lax.fori_loop(0, reps, body, 0)

    def raise_after(k):
        u, part = k // parts, k % parts
        if u == units - 1:
            raise_some(u, part, part + 1)
        elif part == parts - 1:
            raise_some(u, 0, parts)

    acc_buf[...] = jnp.zeros_like(acc_buf)
    begin = FIRST_LAG * FAR + 1
    known = begin + CHUNKS
    used = begin + SECOND_LAG * FAR + 1
    side_end = known + SIDE_LAG * FAR
    assert side_end <= used + CHUNKS - 1
    for s in range(1, used + CHUNKS):
        def gather_step(m, s=s):
            first.step(s, m)
            first_side.step(s - 1, m)

        at.by_class(gather_step)
        if begin <= s < begin + CHUNKS:
            project(s - begin)
        at.by_class(lambda m, s=s: second.step(s - begin, m))
        if s == begin + 1:
            first_side.ready(0)
            lax.fori_loop(0, groups, pick_body, 0)
        if s == known - 1:
            finish()
        at.by_class(lambda m, s=s: second_side.step(s - known + 1, m))
        if used <= s < used + CHUNKS:
            take(s - used)
            if s == used + CHUNKS - 1:
                second_side.ready(0)
                lax.fori_loop(0, groups, weigh_body, 0)
            raise_after(s - used)

    first.drain()
    first_side.drain()

    def lower_chunk(k):
        down_copy(k).wait()
        for j in range(reps):
            half = hidden_units // 2
            result = jnp.dot(act_buf[2 * j], down_ring[k % DOWN_RING, j, :half], preferred_element_type=f32)
            result += jnp.dot(act_buf[2 * j + 1], down_ring[k % DOWN_RING, j, half:], preferred_element_type=f32)
            result = (result * weight_buf[j, :, :1]).astype(bf16)
            for g in range(groups):
                some = result[g * seats : (g + 1) * seats]
                result_buf[g, j * seats : (j + 1) * seats] = some

        if k + DOWN_RING < CHUNKS:
            down_copy(k + DOWN_RING).start()

        def body(g, carry):
            summed = jnp.dot(place_buf[g], result_buf[g], preferred_element_type=f32).astype(bf16)
            proj_buf[pl.ds(k * blocks + g * GROUP, GROUP)] = summed.reshape(GROUP, tok_rows, chunk)
            return carry

        lax.fori_loop(0, groups, body, 0)

    def to_twin(k, half):
        return remote(
            proj_buf.at[pl.ds(k * blocks + (half * 2 + 1 - c) * 8, 8)],
            core_buf.at[pl.ds(k * 16 + half * 8, 8)],
            twin_sem,
            twin_recv.at[k, half],
            at.twin(),
        )

    def line_slot(k, q, far):
        before = sum(4 * LINE if chunk_kind(i)[0] else LINE for i in range(k))
        return before + q * LINE + at.z_of(far)

    def end_slot(k, q):
        return sum(4 if chunk_kind(i)[0] else 1 for i in range(k)) + q

    hop_count = [0, 0]

    def join(k, q, far, m):
        along_z, p = chunk_kind(k)
        target_z = at.z_of(far)
        in_plane = far == m or not along_z
        children = []
        if q == 1 and in_plane:
            children.append((diag_buf.at[k * LINE + target_z], diag_recv.at[k, target_z]))
        if q == 0 and in_plane:
            children.append((a_buf.at[k * LINE + target_z], a_recv.at[k, target_z]))
            children.append((b_buf.at[k * LINE + target_z], b_recv.at[k, target_z]))
        if q == 0 or along_z:
            if far <= m or m > 0:
                slot = line_slot(k, q, far)
                children.append((line_buf.at[slot], line_recv.at[slot]))
            if far == m and m > 0:
                slot = end_slot(k, q)
                children.append((line_end.at[slot], end_recv.at[slot]))
        held = core_buf.at[k * 16 + at.seat(q, far, p)]
        for ref, sem in children:
            remote(ref, ref, hop_sem, sem, at.twin()).wait_recv()
        total = held[...].astype(f32) + proj_buf[k * blocks + at.block(q, far, p)].astype(f32)
        for ref, _ in children:
            total += ref[...].astype(f32)
        if q == 0 and far == m:
            out_ref[:, k * chunk : (k + 1) * chunk] = (res_buf[k] + total).astype(bf16)
            return
        held[...] = total.astype(bf16)
        if q and in_plane:
            buf, sem = {1: (a_buf, a_recv), 2: (b_buf, b_recv), 3: (diag_buf, diag_recv)}[q]
            dst, recv = buf.at[k * LINE + target_z], sem.at[k, target_z]
            target = at.over(1 if q == 1 else 2, p)
        else:
            target = at.line(1 if far > m else -1)
            if m == 0 and far == 1:
                slot = end_slot(k, q)
                dst, recv = line_end.at[slot], end_recv.at[slot]
            else:
                slot = line_slot(k, q, far)
                dst, recv = line_buf.at[slot], line_recv.at[slot]
        remote(held, dst, hop_sem, recv, target).start()
        hop_count[m] += 1

    def join_step(s, m):
        for reach in range(LINE + 1, -1, -1):
            for q in (3, 1, 2, 0):
                for far in range(LINE - 1, -1, -1):
                    for k in range(CHUNKS):
                        if hops(q, far, m) == reach and s - 1 == k + THIRD_LAG * (FAR - reach):
                            join(k, q, far, m)

    for s in range(CHUNKS + THIRD_LAG * FAR + 1):
        if s < CHUNKS:
            lower_chunk(s)
            for half in range(2):
                to_twin(s, half).start()
        if 1 <= s <= CHUNKS:
            for half in range(2):
                to_twin(s - 1, half).wait_recv()
        at.by_class(lambda m: join_step(s, m))

    def hop_drain(m):
        items = core_buf.at[pl.ds(0, hop_count[m])]
        remote(items, items, hop_sem, a_recv.at[0, 0], at.twin()).wait_send()

    at.by_class(hop_drain)
    items = core_buf.at[pl.ds(0, CHUNKS * 16)]
    remote(items, items, twin_sem, twin_recv.at[0, 0], at.twin()).wait_send()
    second.drain()
    second_side.drain()


def run_layer(
    hidden_in, context, out_proj, norm_gain, router, expert_ids, replica_expert, split_pick, up_gate, down
):
    tok_rows, width = hidden_in.shape
    top = expert_ids.shape[1]
    replica_total = replica_expert.shape[0]
    expert_total = router.shape[1]
    reps, hidden_units, _ = down.shape
    blocks = lax.axis_size("dp") * lax.axis_size("expert")
    capacity = max(2, 2 * tok_rows * top // replica_total)
    chunk = width // CHUNKS
    groups = blocks // GROUP
    seats = GROUP * capacity
    slots = reps * seats
    dma = pltpu.SemaphoreType.DMA
    vmem, anywhere = pl.BlockSpec(memory_space=pltpu.VMEM), pl.BlockSpec(memory_space=pl.ANY)

    def spread_sems(chunks):
        return [dma, dma, dma((chunks, 16)), dma((chunks, 2))]

    lines = sum(4 if chunk_kind(k)[0] else 1 for k in range(CHUNKS))
    bf16, f32 = jnp.bfloat16, jnp.float32
    plan = (tok_rows, width, top, capacity, reps, replica_total, expert_total, hidden_units, blocks)
    return pl.pallas_call(
        functools.partial(layer_kernel, plan),
        out_shape=jax.ShapeDtypeStruct((tok_rows, width), bf16),
        in_specs=[vmem, vmem, anywhere, vmem, vmem, vmem, vmem, vmem, anywhere, anywhere],
        out_specs=vmem,
        scratch_shapes=[
            pltpu.VMEM((CHUNKS * blocks, tok_rows, chunk), bf16),
            pltpu.VMEM((CHUNKS * blocks, tok_rows, chunk), bf16),
            pltpu.VMEM((blocks, ROUTE_ROWS + 2 * top, SIDE), bf16),
            pltpu.VMEM((blocks, 4 * top, SIDE), bf16),
            pltpu.VMEM((CHUNKS, tok_rows, chunk), f32),
            pltpu.VMEM((RING, hidden_units // 2, 2 * hidden_units), bf16),
            pltpu.VMEM((DOWN_RING, reps, hidden_units, chunk), bf16),
            pltpu.VMEM((reps, groups * seats, 2 * hidden_units), f32),
            pltpu.VMEM((2 * reps, groups * seats, hidden_units // 2), bf16),
            pltpu.VMEM((groups, slots, GROUP * tok_rows), bf16),
            pltpu.VMEM((groups, GROUP * tok_rows, slots), bf16),
            pltpu.VMEM((reps, groups * seats, SIDE), f32),
            pltpu.VMEM((groups, slots, chunk), bf16),
            pltpu.VMEM((CHUNKS * 16, tok_rows, chunk), bf16),
            pltpu.VMEM((CHUNKS * LINE, tok_rows, chunk), bf16),
            pltpu.VMEM((CHUNKS * LINE, tok_rows, chunk), bf16),
            pltpu.VMEM((CHUNKS * LINE, tok_rows, chunk), bf16),
            pltpu.VMEM((lines * LINE, tok_rows, chunk), bf16),
            pltpu.VMEM((lines, tok_rows, chunk), bf16),
            pltpu.VMEM((reps, groups * seats, SIDE), f32),
            dma((CHUNKS,)),
            dma((RING,)),
            dma((DOWN_RING,)),
        ]
        + spread_sems(CHUNKS)
        + spread_sems(CHUNKS)
        + spread_sems(1)
        + spread_sems(1)
        + [
            dma,
            dma((CHUNKS, 2)),
            dma,
            dma((CHUNKS, LINE)),
            dma((CHUNKS, LINE)),
            dma((CHUNKS, LINE)),
            dma((lines * LINE,)),
            dma((lines,)),
        ],
        compiler_params=pltpu.CompilerParams(collective_id=0, has_side_effects=True, vmem_limit_bytes=62 << 20),
    )(
        hidden_in, context, out_proj, norm_gain.reshape(1, width), router, expert_ids.T,
        replica_expert.reshape(1, replica_total), split_pick.T, up_gate, down,
    )


def solution(mesh):
    plan = run_layer if (mesh.shape["dp"], mesh.shape["expert"]) == (4, 8) else per_device
    return jax.shard_map(
        plan,
        mesh=mesh,
        in_specs=(
            P(("dp", "expert"), None),
            P(("dp", "expert"), None),
            P(("dp", "expert"), None),
            P(),
            P(("dp", "expert"), None),
            P(("dp", "expert"), None),
            P(),
            P(("dp", "expert"), None),
            P(("dp", "expert"), None, None),
            P(("dp", "expert"), None, None),
        ),
        out_specs=P(("dp", "expert"), None),
        check_vma=False,
    )
```

```python
import functools

import jax
import jax.numpy as jnp
from jax import lax
from jax.experimental import pallas as pl
from jax.experimental.pallas import tpu as pltpu
from jax.sharding import PartitionSpec as P


def rms_norm(residual, norm_gain):
    scale_back = lax.rsqrt(jnp.mean(residual * residual, axis=-1, keepdims=True) + 1e-05)
    return (residual * scale_back * norm_gain).astype(jnp.bfloat16)


def route_block(expert_ids, split_pick, replica_expert):
    replica_total = replica_expert.shape[0]
    replica_iota = lax.iota(jnp.int32, replica_total)
    same_expert = replica_expert[:, None] == replica_expert[None, :]
    earlier = replica_iota[:, None] > replica_iota[None, :]
    replica_rank = jnp.sum((same_expert & earlier).astype(jnp.int32), axis=1)
    serves = expert_ids[:, :, None] == replica_expert[None, None, :]
    replica_count = jnp.sum(serves.astype(jnp.int32), axis=-1)
    wanted = split_pick % replica_count
    matches = serves & (replica_rank[None, None, :] == wanted[:, :, None])
    replica = jnp.sum(jnp.where(matches, replica_iota[None, None, :], 0), axis=-1)
    flat_replica = replica.reshape(-1)
    pair_iota = lax.iota(jnp.int32, flat_replica.shape[0])
    same_target = flat_replica[:, None] == flat_replica[None, :]
    before = pair_iota[:, None] > pair_iota[None, :]
    slot_index = jnp.sum((same_target & before).astype(jnp.int32), axis=1)
    return (replica, slot_index.reshape(replica.shape))


def apply_experts(incoming, up_gate, down, capacity):
    arrived_shape = incoming.shape
    local_reps = up_gate.shape[0]
    hidden_units = down.shape[1]
    stacked = incoming.reshape(-1, local_reps, capacity, incoming.shape[-1])
    gate_up = jnp.einsum("sjcd,jdf->sjcf", stacked, up_gate, preferred_element_type=jnp.float32)
    hidden_act = (jax.nn.silu(gate_up[..., :hidden_units]) * gate_up[..., hidden_units:]).astype(
        jnp.bfloat16
    )
    expert_out = jnp.einsum("sjcf,jfd->sjcd", hidden_act, down, preferred_element_type=jnp.float32)
    return expert_out.astype(jnp.bfloat16).reshape(arrived_shape)


def per_device(
    hidden_in,
    context,
    out_proj,
    norm_gain,
    router,
    expert_ids,
    replica_expert,
    split_pick,
    up_gate,
    down,
):
    tok_rows, model_width = hidden_in.shape
    top_count = expert_ids.shape[1]
    replica_total = replica_expert.shape[0]
    local_reps = up_gate.shape[0]
    data_groups = lax.axis_size("dp")
    expert_groups = lax.axis_size("expert")
    capacity = max(2, 2 * tok_rows * top_count // replica_total)
    summed = jnp.dot(
        context,
        lax.all_gather(out_proj, ("dp", "expert"), axis=0, tiled=True),
        preferred_element_type=jnp.float32,
    )
    router_rows = lax.all_gather(router, ("dp", "expert"), axis=0, tiled=True)
    residual = hidden_in.astype(jnp.float32) + summed
    normed = rms_norm(residual, norm_gain)
    logits = jnp.dot(normed, router_rows, preferred_element_type=jnp.float32)
    hit_mask = expert_ids[:, :, None] == lax.iota(jnp.int32, logits.shape[1])[None, None, :]
    chosen = jnp.sum(jnp.where(hit_mask, logits[:, None, :], 0.0), axis=-1)
    raised = jnp.exp(chosen)
    route_weight = raised / jnp.sum(raised, axis=-1, keepdims=True)
    replica, slot_index = route_block(expert_ids, split_pick, replica_expert)
    within_cap = slot_index < capacity
    buffer_row = jnp.where(within_cap, replica * capacity + slot_index, -1).reshape(-1)
    slot_total = replica_total * capacity
    matches = buffer_row[None, :] == lax.iota(jnp.int32, slot_total)[:, None]
    filled = jnp.any(matches, axis=1)
    row_of_pair = lax.iota(jnp.int32, tok_rows * top_count) // top_count
    anchor = jnp.sum(jnp.where(matches, row_of_pair[None, :], 0), axis=1)
    outgoing = jnp.where(filled[:, None], normed[anchor], jnp.zeros((), jnp.bfloat16))
    outgoing = outgoing.reshape(data_groups, expert_groups, local_reps * capacity, model_width)
    incoming = lax.all_to_all(
        lax.all_to_all(outgoing, "expert", split_axis=1, concat_axis=1, tiled=True),
        "dp",
        split_axis=0,
        concat_axis=0,
        tiled=True,
    )
    results = apply_experts(incoming, up_gate, down, capacity)
    returned = lax.all_to_all(
        lax.all_to_all(results, "dp", split_axis=0, concat_axis=0, tiled=True),
        "expert",
        split_axis=1,
        concat_axis=1,
        tiled=True,
    )
    returned = returned.reshape(slot_total, model_width)
    safe_index = jnp.where(within_cap, replica * capacity + slot_index, 0)
    gathered = returned[safe_index]
    kept_weight = jnp.where(within_cap, route_weight, 0.0)
    layer_out = residual + jnp.sum(kept_weight[:, :, None] * gathered.astype(jnp.float32), axis=1)
    return layer_out.astype(jnp.bfloat16)

MESH = pl.DeviceIdType.MESH
LINE = 4
SIDE = 128
CHUNKS = 4
FAR = LINE + 1
FIRST_LAG = 1
SECOND_LAG = 1
THIRD_LAG = 1
SIDE_LAG = 1
FIRST_LEAD = 1
SECOND_LEAD = 0
ROUTE_ROWS = 32
RING = 4
DOWN_RING = 2
GROUP = 4


def place():
    d, e = lax.axis_index("dp"), lax.axis_index("expert")
    return d // 2, d % 2, e // 2, e % 2


def device_of(y, c, z, x):
    return (y * 2 + c, z * 2 + x)


def block_of(y, c, z, x):
    return (y * 2 + c) * (2 * LINE) + z * 2 + x


def greet(barrier, y, c, z, x):
    for other in (device_of(y, 1 - c, z, x), device_of(1 - y, c, z, x), device_of(y, c, z, 1 - x)):
        pl.semaphore_signal(barrier, inc=1, device_id=other, device_id_type=MESH)

    @pl.when(z > 0)
    def _():
        pl.semaphore_signal(barrier, inc=1, device_id=device_of(y, c, z - 1, x), device_id_type=MESH)

    @pl.when(z < LINE - 1)
    def _():
        pl.semaphore_signal(barrier, inc=1, device_id=device_of(y, c, z + 1, x), device_id_type=MESH)

    pl.semaphore_wait(barrier, 3 + jnp.minimum(z, 1) + jnp.minimum(LINE - 1 - z, 1))


def plane_shift(q, p):
    qa, qb = q & 1, q >> 1
    return qb * (1 - p) + qa * p, qa * (1 - p) + qb * p


def chunk_kind(k):
    return k % 4 == 1, (3 * (k // 4) + (k % 4 + 1) // 2) % 2


def side_kind(k):
    return False, 1


def hops(q, far, m):
    return abs(far - m) + (q & 1) + (q >> 1)


class Place:
    def __init__(self):
        self.y, self.c, self.z, self.x = place()
        self.flip = self.z // 2
        self.m = self.z + self.flip * (LINE - 1 - 2 * self.z)
        self.outward = 1 - 2 * self.flip

    def z_of(self, far):
        return far + self.flip * (LINE - 1 - 2 * far)

    def plane(self, q, p):
        dy, dx = plane_shift(q, p)
        return (self.y + dy) % 2 if dy else self.y, (self.x + dx) % 2 if dx else self.x

    def seat(self, q, far, p):
        y, x = self.plane(q, p)
        return y * (2 * LINE) + self.z_of(far) * 2 + x

    def block(self, q, far, p):
        y, x = self.plane(q, p)
        return block_of(y, self.c, self.z_of(far), x)

    def over(self, q, p):
        y, x = self.plane(q, p)
        return device_of(y, self.c, self.z, x)

    def line(self, way):
        return device_of(self.y, self.c, self.z + way * self.outward, self.x)

    def twin(self):
        return device_of(self.y, 1 - self.c, self.z, self.x)

    def by_class(self, act):
        for m in range(2):
            @pl.when(self.m == m)
            def _(m=m):
                act(m)


def remote(src, dst, send_sem, recv_sem, target):
    return pltpu.make_async_remote_copy(
        src_ref=src, dst_ref=dst, send_sem=send_sem, recv_sem=recv_sem, device_id=target, device_id_type=MESH
    )


class Spread:
    def __init__(self, lag, lead, at, chunks, buf, blocks, kind, line_sem, twin_sem, recv_sem, twin_recv):
        self.at, self.chunks, self.buf, self.blocks, self.kind = at, chunks, buf, blocks, kind
        self.line_sem, self.twin_sem, self.recv_sem, self.twin_recv = line_sem, twin_sem, recv_sem, twin_recv
        self.sent = [0, 0]
        self.lag, self.lead = lag, lead

    def item(self, k, block):
        return self.buf.at[k * self.blocks + block]

    def event(self, k, q, far, m):
        at = self.at
        along_z, p = self.kind(k)
        item, recv = self.item(k, at.block(q, far, p)), self.recv_sem.at[k, at.seat(q, far, p)]
        targets = []
        if q == 0 or along_z:
            if far <= m:
                targets.append(at.line(1))
            if m > 0 and far >= m:
                targets.append(at.line(-1))
        if far == m or not along_z:
            if q <= 1:
                targets.append(at.over(2, p))
            if q == 0:
                targets.append(at.over(1, p))
        if q or far != m:
            remote(item, item, self.line_sem, recv, at.twin()).wait_recv()
        for target in targets:
            remote(item, item, self.line_sem, recv, target).start()
        self.sent[m] += len(targets)

    def twin(self, k, half, core):
        items = self.buf.at[pl.ds(k * self.blocks + (half * 2 + core) * 8, 8)]
        return remote(items, items, self.twin_sem, self.twin_recv.at[k, half], self.at.twin())

    def step(self, s, m):
        for reach in range(LINE + 2):
            for far in range(LINE):
                for q in range(4):
                    k = s - self.lag * reach + (self.lead if reach == 0 else 0)
                    if hops(q, far, m) != reach:
                        continue
                    if reach == 0 and s == 0:
                        for early in range(min(k, self.chunks)):
                            self.event(early, q, far, m)
                    if 0 <= k < self.chunks:
                        self.event(k, q, far, m)
        k = s - self.lag * (FAR - m)
        if 0 <= k < self.chunks:
            for half in range(2):
                self.twin(k, half, self.at.c).start()

    def ready(self, k):
        for half in range(2):
            self.twin(k, half, 1 - self.at.c).wait_recv()

    def drain(self):
        def act(m):
            items = self.buf.at[pl.ds(0, self.sent[m])]
            remote(items, items, self.line_sem, self.recv_sem.at[0, 0], self.at.twin()).wait_send()

        self.at.by_class(act)
        items = self.buf.at[pl.ds(0, self.chunks * 16)]
        remote(items, items, self.twin_sem, self.twin_recv.at[0, 0], self.at.twin()).wait_send()


def layer_kernel(
    plan, hid_ref, ctx_ref, proj_ref, gain_ref, router_ref, ids_ref, rep_ref, split_ref, up_ref, down_ref,
    out_ref, proj_buf, norm_buf, side_buf, weight_side, res_buf, up_ring, down_ring, acc_buf, act_buf, pick_buf,
    place_buf, weight_buf, result_buf, core_buf, a_buf, b_buf, diag_buf, line_buf, line_end, scale_buf, local_sem, up_load,
    down_load, *sems
):
    tok_rows, width, top, capacity, reps, replica_total, expert_total, hidden_units, blocks = plan
    at = Place()
    y, c, z, x = at.y, at.c, at.z, at.x
    me = block_of(y, c, z, x)
    chunk = width // CHUNKS
    groups = blocks // GROUP
    group_rows = GROUP * tok_rows
    seats = GROUP * capacity
    slots = reps * seats
    parts = hidden_units // 2 // chunk
    unit = parts * chunk
    units = width // unit
    f32, bf16 = jnp.float32, jnp.bfloat16

    def own_copy(k):
        return pltpu.make_async_copy(
            proj_ref.at[:, pl.ds(k * chunk, chunk)], proj_buf.at[k * blocks + me], local_sem.at[k]
        )

    def up_copy(i):
        u, j = i // reps, i % reps
        return pltpu.make_async_copy(
            up_ref.at[j, pl.ds(u * unit if isinstance(u, int) else pl.multiple_of(u * unit, unit), unit)], up_ring.at[i % RING], up_load.at[i % RING]
        )

    def down_copy(k):
        return pltpu.make_async_copy(
            down_ref.at[:, :, pl.ds(k * chunk, chunk)],
            down_ring.at[k % DOWN_RING],
            down_load.at[k % DOWN_RING],
        )

    for k in range(CHUNKS):
        own_copy(k).start()
    greet(pltpu.get_barrier_semaphore(), y, c, z, x)
    for i in range(RING):
        up_copy(i).start()
    for k in range(DOWN_RING):
        down_copy(k).start()

    first = Spread(FIRST_LAG, FIRST_LEAD, at, CHUNKS, proj_buf, blocks, chunk_kind, *sems[0:4])
    second = Spread(SECOND_LAG, SECOND_LEAD, at, CHUNKS, norm_buf, blocks, chunk_kind, *sems[4:8])
    first_side = Spread(FIRST_LAG, 0, at, 1, side_buf, blocks, side_kind, *sems[8:12])
    second_side = Spread(SIDE_LAG, 0, at, 1, weight_side, blocks, side_kind, *sems[12:16])
    twin_sem, twin_recv, hop_sem, a_recv, b_recv, diag_recv, line_recv, end_recv = sems[16:]

    for k in range(CHUNKS):
        own_copy(k).wait()
    at.by_class(lambda m: first.step(0, m))

    rep_row = jnp.broadcast_to(rep_ref[...], (replica_total, replica_total))
    row_i = lax.broadcasted_iota(jnp.int32, (replica_total, replica_total), 0)
    col_i = lax.broadcasted_iota(jnp.int32, (replica_total, replica_total), 1)
    rep_col = jnp.sum(jnp.where(row_i == col_i, rep_row, 0), axis=1, keepdims=True)
    rank = jnp.sum(jnp.where((rep_row == rep_col) & (col_i < row_i), 1, 0), axis=1, keepdims=True)
    replica_i = lax.broadcasted_iota(jnp.int32, (replica_total, tok_rows), 0)
    taken = jnp.zeros((replica_total, tok_rows), f32)
    hits, replicas = [], []
    for k in range(top):
        serves = rep_col == ids_ref[k : k + 1, :]
        count = jnp.sum(jnp.where(serves, 1.0, 0.0), axis=0, keepdims=True)
        pick = split_ref[k : k + 1, :].astype(f32)
        wanted = pick - jnp.floor((pick + 0.5) / count) * count
        hit = serves & (rank.astype(f32) == wanted)
        hits.append(hit)
        taken = jnp.where(hit, 1.0, taken)
        replicas.append(jnp.sum(jnp.where(hit, replica_i, 0).astype(f32), axis=0, keepdims=True))
    tok_i = lax.broadcasted_iota(jnp.int32, (tok_rows, tok_rows), 0)
    tok_j = lax.broadcasted_iota(jnp.int32, (tok_rows, tok_rows), 1)
    before = jnp.where(tok_i < tok_j, 1.0, 0.0).astype(bf16)
    earlier = jnp.dot(taken.astype(bf16), before, preferred_element_type=f32)
    slot_rows = [
        jnp.minimum(jnp.sum(jnp.where(hit, earlier, 0.0), axis=0, keepdims=True), float(capacity)) for hit in hits
    ]
    wide_i = lax.broadcasted_iota(jnp.int32, (tok_rows, SIDE), 0)
    wide_j = lax.broadcasted_iota(jnp.int32, (tok_rows, SIDE), 1)
    widen = jnp.where(wide_j == wide_i + x * tok_rows, 1.0, 0.0).astype(bf16)
    routing = jnp.concatenate(replicas + slot_rows, axis=0).astype(bf16)
    side_buf[me, ROUTE_ROWS:] = jnp.dot(routing, widen, preferred_element_type=f32).astype(bf16)
    half_i = lax.broadcasted_iota(jnp.int32, (expert_total, SIDE), 0)
    half_j = lax.broadcasted_iota(jnp.int32, (expert_total, SIDE), 1)
    packed = jnp.zeros((ROUTE_ROWS, SIDE), f32)
    for h in range(2):
        to_half = jnp.where(half_j == half_i + h * expert_total, 1.0, 0.0).astype(bf16)
        packed += jnp.dot(
            router_ref[h * ROUTE_ROWS : (h + 1) * ROUTE_ROWS, :], to_half, preferred_element_type=f32
        )
    side_buf[me, :ROUTE_ROWS] = packed.astype(bf16)

    def project(k):
        first.ready(k)
        weights = proj_buf[k * blocks : (k + 1) * blocks].reshape(width, chunk)
        summed = jnp.dot(ctx_ref[...], weights, preferred_element_type=f32)
        residual = hid_ref[:, k * chunk : (k + 1) * chunk].astype(f32) + summed
        res_buf[k] = residual
        norm_buf[k * blocks + me] = (residual * gain_ref[:, k * chunk : (k + 1) * chunk]).astype(bf16)

    def finish():
        square = jnp.zeros((tok_rows, 1), f32)
        for k in range(CHUNKS):
            square += jnp.sum(res_buf[k] * res_buf[k], axis=1, keepdims=True)
        scale_back = lax.rsqrt(square / width + 1e-05)
        low_logits = jnp.zeros((tok_rows, SIDE), f32)
        high_logits = low_logits
        share = chunk // tok_rows
        in_low = lax.broadcasted_iota(jnp.int32, (tok_rows, chunk), 1) % tok_rows < ROUTE_ROWS
        for k in range(CHUNKS):
            gain = gain_ref[:, k * chunk : (k + 1) * chunk]
            own = (res_buf[k] * scale_back * gain).astype(bf16).astype(f32)
            rows = side_buf[k * share : (k + 1) * share, :ROUTE_ROWS]
            rows = jnp.concatenate([rows, rows], axis=1).reshape(chunk, SIDE)
            low_logits += jnp.dot(jnp.where(in_low, own, 0.0).astype(bf16), rows, preferred_element_type=f32)
            high_logits += jnp.dot(jnp.where(in_low, 0.0, own).astype(bf16), rows, preferred_element_type=f32)
        logits = low_logits.T[:expert_total] + high_logits.T[expert_total:]
        expert_i = lax.broadcasted_iota(jnp.int32, (expert_total, tok_rows), 0)
        raised = [
            jnp.exp(jnp.sum(jnp.where(expert_i == ids_ref[k : k + 1, :], logits, 0.0), axis=0, keepdims=True))
            for k in range(top)
        ]
        raised = jnp.concatenate(raised, axis=0)
        route_weight = raised / jnp.sum(raised, axis=0, keepdims=True)
        upper = route_weight.astype(bf16).astype(f32)
        scale_row = jnp.broadcast_to(scale_back, (tok_rows, SIDE)).T[:1]
        scale_top = scale_row.astype(bf16).astype(f32)
        rest = jnp.zeros((2 * top - 2, tok_rows), f32)
        sent = jnp.concatenate([upper, route_weight - upper, scale_top, scale_row - scale_top, rest], axis=0).astype(bf16)
        weight_side[me] = jnp.dot(sent, widen, preferred_element_type=f32).astype(bf16)

    lane = lax.broadcasted_iota(jnp.int32, (1, group_rows), 1)
    slot_i = lax.broadcasted_iota(jnp.int32, (slots, group_rows), 0).astype(f32)
    seat_base = (lane // tok_rows * capacity).astype(f32)
    low = (me * reps).astype(f32)

    def group_side(ref, g, start, stop):
        def pair(i):
            return ref[GROUP * g + i, start:stop].astype(f32) + ref[GROUP * g + i + 1, start:stop].astype(f32)

        return jnp.concatenate([pair(0), pair(2)], axis=1)

    def seats_of(g):
        routed = group_side(side_buf, g, ROUTE_ROWS, ROUTE_ROWS + 2 * top)
        replica = routed[:top] - low
        slot = routed[top:]
        here = (replica >= 0) & (replica < reps) & (slot < capacity)
        return jnp.where(here, replica * seats + seat_base + slot, -1.0)

    def pick_body(g, carry):
        seat = seats_of(g)
        picked = jnp.zeros((slots, group_rows), f32)
        for k in range(top):
            picked = jnp.where(slot_i == seat[k : k + 1], 1.0, picked)
        pick_buf[g] = picked.astype(bf16)
        place_buf[g] = picked.T.astype(bf16)
        return carry

    def weigh_body(g, carry):
        seat = seats_of(g)
        weights = group_side(weight_side, g, 0, 2 * top)
        weights = weights[:top] + weights[top:]
        weighed = jnp.zeros((slots, group_rows), f32)
        for k in range(top):
            weighed = jnp.where(slot_i == seat[k : k + 1], weights[k : k + 1], weighed)
        weight = jnp.sum(weighed, axis=1, keepdims=True)
        scales = group_side(weight_side, g, 2 * top, 2 * top + 2)
        scale = jnp.sum(pick_buf[g].astype(f32) * (scales[:1] + scales[1:]), axis=1, keepdims=True)
        for j in range(reps):
            rows = pl.ds(pl.multiple_of(g * seats, seats), seats)
            scale_buf[j, rows] = jnp.broadcast_to(scale[j * seats : (j + 1) * seats], (seats, SIDE))
            weight_buf[j, rows] = jnp.broadcast_to(weight[j * seats : (j + 1) * seats], (seats, SIDE))
        return carry

    def take(k):
        second.ready(k)

        def body(g, carry):
            rows = norm_buf[pl.ds(k * blocks + g * GROUP, GROUP)].reshape(group_rows, chunk)
            taken = jnp.dot(pick_buf[g], rows, preferred_element_type=f32).astype(bf16)
            for j in range(reps):
                act_buf[
                    (k // parts % 2) * reps + j,
                    pl.ds(pl.multiple_of(g * seats, seats), seats),
                    (k % parts) * chunk : (k % parts + 1) * chunk,
                ] = taken[j * seats : (j + 1) * seats]
            return carry

        lax.fori_loop(0, groups, body, 0, unroll=True)

    def activate(j):
        scale = scale_buf[j, :, :1]
        for h in range(2):
            half = hidden_units // 2
            gate = acc_buf[j, :, h * half : (h + 1) * half] * scale
            raised = acc_buf[j, :, hidden_units + h * half : hidden_units + (h + 1) * half] * scale
            act_buf[2 * j + h] = (gate / (1.0 + jnp.exp(-gate)) * raised).astype(bf16)

    def raise_some(u, start, stop):
        depth = slice(start * chunk, stop * chunk)

        last = u == units - 1 and stop == parts

        def body(j, carry):
            i = u * reps + j
            if last and j:
                activate(j - 1)
            if start == 0:
                up_copy(i).wait()
            expert_in = act_buf[(u % 2) * reps + j, :, depth]
            for t in range(4):
                columns = slice(t * (2 * hidden_units // 4), (t + 1) * (2 * hidden_units // 4))
                acc_buf[j, :, columns] += jnp.dot(
                    expert_in, up_ring[i % RING, depth, columns], preferred_element_type=f32
                )
            if stop == parts and u < units - 1:
                up_copy(i + RING).start()
            return carry

        if last:
            for j in range(reps):
                body(j, 0)
            activate(reps - 1)
        else:
            lax.fori_loop(0, reps, body, 0)

    def raise_after(k):
        u, part = k // parts, k % parts
        if u == units - 1:
            raise_some(u, part, part + 1)
        elif part == parts - 1:
            raise_some(u, 0, parts)

    acc_buf[...] = jnp.zeros_like(acc_buf)
    begin = FIRST_LAG * FAR + 1
    known = begin + CHUNKS
    used = begin + SECOND_LAG * FAR + 1
    side_end = known + SIDE_LAG * FAR
    assert side_end <= used + CHUNKS - 1
    for s in range(1, used + CHUNKS):
        def gather_step(m, s=s):
            first.step(s, m)
            first_side.step(s - 1, m)

        at.by_class(gather_step)
        if begin <= s < begin + CHUNKS:
            project(s - begin)
        at.by_class(lambda m, s=s: second.step(s - begin, m))
        if s == begin + 1:
            first_side.ready(0)
            lax.fori_loop(0, groups, pick_body, 0)
        if s == known - 1:
            finish()
        at.by_class(lambda m, s=s: second_side.step(s - known + 1, m))
        if used <= s < used + CHUNKS:
            take(s - used)
            if s == used + CHUNKS - 1:
                second_side.ready(0)
                lax.fori_loop(0, groups, weigh_body, 0)
            raise_after(s - used)

    first.drain()
    first_side.drain()

    def lower_chunk(k):
        down_copy(k).wait()
        for j in range(reps):
            half = hidden_units // 2
            result = jnp.dot(act_buf[2 * j], down_ring[k % DOWN_RING, j, :half], preferred_element_type=f32)
            result += jnp.dot(act_buf[2 * j + 1], down_ring[k % DOWN_RING, j, half:], preferred_element_type=f32)
            result = (result * weight_buf[j, :, :1]).astype(bf16)
            for g in range(groups):
                some = result[g * seats : (g + 1) * seats]
                result_buf[g, j * seats : (j + 1) * seats] = some

        if k + DOWN_RING < CHUNKS:
            down_copy(k + DOWN_RING).start()

        def body(g, carry):
            summed = jnp.dot(place_buf[g], result_buf[g], preferred_element_type=f32).astype(bf16)
            proj_buf[pl.ds(k * blocks + g * GROUP, GROUP)] = summed.reshape(GROUP, tok_rows, chunk)
            return carry

        lax.fori_loop(0, groups, body, 0, unroll=True)

    def to_twin(k, half):
        return remote(
            proj_buf.at[pl.ds(k * blocks + (half * 2 + 1 - c) * 8, 8)],
            core_buf.at[pl.ds(k * 16 + half * 8, 8)],
            twin_sem,
            twin_recv.at[k, half],
            at.twin(),
        )

    def line_slot(k, q, far):
        before = sum(4 * LINE if chunk_kind(i)[0] else LINE for i in range(k))
        return before + q * LINE + at.z_of(far)

    def end_slot(k, q):
        return sum(4 if chunk_kind(i)[0] else 1 for i in range(k)) + q

    hop_count = [0, 0]

    def join(k, q, far, m):
        along_z, p = chunk_kind(k)
        target_z = at.z_of(far)
        in_plane = far == m or not along_z
        children = []
        if q == 1 and in_plane:
            children.append((diag_buf.at[k * LINE + target_z], diag_recv.at[k, target_z]))
        if q == 0 and in_plane:
            children.append((a_buf.at[k * LINE + target_z], a_recv.at[k, target_z]))
            children.append((b_buf.at[k * LINE + target_z], b_recv.at[k, target_z]))
        if q == 0 or along_z:
            if far <= m or m > 0:
                slot = line_slot(k, q, far)
                children.append((line_buf.at[slot], line_recv.at[slot]))
            if far == m and m > 0:
                slot = end_slot(k, q)
                children.append((line_end.at[slot], end_recv.at[slot]))
        held = core_buf.at[k * 16 + at.seat(q, far, p)]
        for ref, sem in children:
            remote(ref, ref, hop_sem, sem, at.twin()).wait_recv()
        total = held[...].astype(f32) + proj_buf[k * blocks + at.block(q, far, p)].astype(f32)
        for ref, _ in children:
            total += ref[...].astype(f32)
        if q == 0 and far == m:
            out_ref[:, k * chunk : (k + 1) * chunk] = (res_buf[k] + total).astype(bf16)
            return
        held[...] = total.astype(bf16)
        if q and in_plane:
            buf, sem = {1: (a_buf, a_recv), 2: (b_buf, b_recv), 3: (diag_buf, diag_recv)}[q]
            dst, recv = buf.at[k * LINE + target_z], sem.at[k, target_z]
            target = at.over(1 if q == 1 else 2, p)
        else:
            target = at.line(1 if far > m else -1)
            if m == 0 and far == 1:
                slot = end_slot(k, q)
                dst, recv = line_end.at[slot], end_recv.at[slot]
            else:
                slot = line_slot(k, q, far)
                dst, recv = line_buf.at[slot], line_recv.at[slot]
        remote(held, dst, hop_sem, recv, target).start()
        hop_count[m] += 1

    def join_step(s, m):
        for reach in range(LINE + 1, -1, -1):
            for q in (3, 1, 2, 0):
                for far in range(LINE - 1, -1, -1):
                    for k in range(CHUNKS):
                        if hops(q, far, m) == reach and s - 1 == k + THIRD_LAG * (FAR - reach):
                            join(k, q, far, m)

    for s in range(CHUNKS + THIRD_LAG * FAR + 1):
        if s < CHUNKS:
            lower_chunk(s)
            for half in range(2):
                to_twin(s, half).start()
        if 1 <= s <= CHUNKS:
            for half in range(2):
                to_twin(s - 1, half).wait_recv()
        at.by_class(lambda m: join_step(s, m))

    def hop_drain(m):
        items = core_buf.at[pl.ds(0, hop_count[m])]
        remote(items, items, hop_sem, a_recv.at[0, 0], at.twin()).wait_send()

    at.by_class(hop_drain)
    items = core_buf.at[pl.ds(0, CHUNKS * 16)]
    remote(items, items, twin_sem, twin_recv.at[0, 0], at.twin()).wait_send()
    second.drain()
    second_side.drain()


def run_layer(
    hidden_in, context, out_proj, norm_gain, router, expert_ids, replica_expert, split_pick, up_gate, down
):
    tok_rows, width = hidden_in.shape
    top = expert_ids.shape[1]
    replica_total = replica_expert.shape[0]
    expert_total = router.shape[1]
    reps, hidden_units, _ = down.shape
    blocks = lax.axis_size("dp") * lax.axis_size("expert")
    capacity = max(2, 2 * tok_rows * top // replica_total)
    chunk = width // CHUNKS
    groups = blocks // GROUP
    seats = GROUP * capacity
    slots = reps * seats
    dma = pltpu.SemaphoreType.DMA
    vmem, anywhere = pl.BlockSpec(memory_space=pltpu.VMEM), pl.BlockSpec(memory_space=pl.ANY)

    def spread_sems(chunks):
        return [dma, dma, dma((chunks, 16)), dma((chunks, 2))]

    lines = sum(4 if chunk_kind(k)[0] else 1 for k in range(CHUNKS))
    bf16, f32 = jnp.bfloat16, jnp.float32
    plan = (tok_rows, width, top, capacity, reps, replica_total, expert_total, hidden_units, blocks)
    return pl.pallas_call(
        functools.partial(layer_kernel, plan),
        out_shape=jax.ShapeDtypeStruct((tok_rows, width), bf16),
        in_specs=[vmem, vmem, anywhere, vmem, vmem, vmem, vmem, vmem, anywhere, anywhere],
        out_specs=vmem,
        scratch_shapes=[
            pltpu.VMEM((CHUNKS * blocks, tok_rows, chunk), bf16),
            pltpu.VMEM((CHUNKS * blocks, tok_rows, chunk), bf16),
            pltpu.VMEM((blocks, ROUTE_ROWS + 2 * top, SIDE), bf16),
            pltpu.VMEM((blocks, 4 * top, SIDE), bf16),
            pltpu.VMEM((CHUNKS, tok_rows, chunk), f32),
            pltpu.VMEM((RING, hidden_units // 2, 2 * hidden_units), bf16),
            pltpu.VMEM((DOWN_RING, reps, hidden_units, chunk), bf16),
            pltpu.VMEM((reps, groups * seats, 2 * hidden_units), f32),
            pltpu.VMEM((2 * reps, groups * seats, hidden_units // 2), bf16),
            pltpu.VMEM((groups, slots, GROUP * tok_rows), bf16),
            pltpu.VMEM((groups, GROUP * tok_rows, slots), bf16),
            pltpu.VMEM((reps, groups * seats, SIDE), f32),
            pltpu.VMEM((groups, slots, chunk), bf16),
            pltpu.VMEM((CHUNKS * 16, tok_rows, chunk), bf16),
            pltpu.VMEM((CHUNKS * LINE, tok_rows, chunk), bf16),
            pltpu.VMEM((CHUNKS * LINE, tok_rows, chunk), bf16),
            pltpu.VMEM((CHUNKS * LINE, tok_rows, chunk), bf16),
            pltpu.VMEM((lines * LINE, tok_rows, chunk), bf16),
            pltpu.VMEM((lines, tok_rows, chunk), bf16),
            pltpu.VMEM((reps, groups * seats, SIDE), f32),
            dma((CHUNKS,)),
            dma((RING,)),
            dma((DOWN_RING,)),
        ]
        + spread_sems(CHUNKS)
        + spread_sems(CHUNKS)
        + spread_sems(1)
        + spread_sems(1)
        + [
            dma,
            dma((CHUNKS, 2)),
            dma,
            dma((CHUNKS, LINE)),
            dma((CHUNKS, LINE)),
            dma((CHUNKS, LINE)),
            dma((lines * LINE,)),
            dma((lines,)),
        ],
        compiler_params=pltpu.CompilerParams(collective_id=0, has_side_effects=True, vmem_limit_bytes=62 << 20),
    )(
        hidden_in, context, out_proj, norm_gain.reshape(1, width), router, expert_ids.T,
        replica_expert.reshape(1, replica_total), split_pick.T, up_gate, down,
    )


def solution(mesh):
    plan = run_layer if (mesh.shape["dp"], mesh.shape["expert"]) == (4, 8) else per_device
    return jax.shard_map(
        plan,
        mesh=mesh,
        in_specs=(
            P(("dp", "expert"), None),
            P(("dp", "expert"), None),
            P(("dp", "expert"), None),
            P(),
            P(("dp", "expert"), None),
            P(("dp", "expert"), None),
            P(),
            P(("dp", "expert"), None),
            P(("dp", "expert"), None, None),
            P(("dp", "expert"), None, None),
        ),
        out_specs=P(("dp", "expert"), None),
        check_vma=False,
    )
```

```python
import functools

import jax
import jax.numpy as jnp
from jax import lax
from jax.experimental import pallas as pl
from jax.experimental.pallas import tpu as pltpu
from jax.sharding import PartitionSpec as P


def rms_norm(residual, norm_gain):
    scale_back = lax.rsqrt(jnp.mean(residual * residual, axis=-1, keepdims=True) + 1e-05)
    return (residual * scale_back * norm_gain).astype(jnp.bfloat16)


def route_block(expert_ids, split_pick, replica_expert):
    replica_total = replica_expert.shape[0]
    replica_iota = lax.iota(jnp.int32, replica_total)
    same_expert = replica_expert[:, None] == replica_expert[None, :]
    earlier = replica_iota[:, None] > replica_iota[None, :]
    replica_rank = jnp.sum((same_expert & earlier).astype(jnp.int32), axis=1)
    serves = expert_ids[:, :, None] == replica_expert[None, None, :]
    replica_count = jnp.sum(serves.astype(jnp.int32), axis=-1)
    wanted = split_pick % replica_count
    matches = serves & (replica_rank[None, None, :] == wanted[:, :, None])
    replica = jnp.sum(jnp.where(matches, replica_iota[None, None, :], 0), axis=-1)
    flat_replica = replica.reshape(-1)
    pair_iota = lax.iota(jnp.int32, flat_replica.shape[0])
    same_target = flat_replica[:, None] == flat_replica[None, :]
    before = pair_iota[:, None] > pair_iota[None, :]
    slot_index = jnp.sum((same_target & before).astype(jnp.int32), axis=1)
    return (replica, slot_index.reshape(replica.shape))


def apply_experts(incoming, up_gate, down, capacity):
    arrived_shape = incoming.shape
    local_reps = up_gate.shape[0]
    hidden_units = down.shape[1]
    stacked = incoming.reshape(-1, local_reps, capacity, incoming.shape[-1])
    gate_up = jnp.einsum("sjcd,jdf->sjcf", stacked, up_gate, preferred_element_type=jnp.float32)
    hidden_act = (jax.nn.silu(gate_up[..., :hidden_units]) * gate_up[..., hidden_units:]).astype(
        jnp.bfloat16
    )
    expert_out = jnp.einsum("sjcf,jfd->sjcd", hidden_act, down, preferred_element_type=jnp.float32)
    return expert_out.astype(jnp.bfloat16).reshape(arrived_shape)


def per_device(
    hidden_in,
    context,
    out_proj,
    norm_gain,
    router,
    expert_ids,
    replica_expert,
    split_pick,
    up_gate,
    down,
):
    tok_rows, model_width = hidden_in.shape
    top_count = expert_ids.shape[1]
    replica_total = replica_expert.shape[0]
    local_reps = up_gate.shape[0]
    data_groups = lax.axis_size("dp")
    expert_groups = lax.axis_size("expert")
    capacity = max(2, 2 * tok_rows * top_count // replica_total)
    summed = jnp.dot(
        context,
        lax.all_gather(out_proj, ("dp", "expert"), axis=0, tiled=True),
        preferred_element_type=jnp.float32,
    )
    router_rows = lax.all_gather(router, ("dp", "expert"), axis=0, tiled=True)
    residual = hidden_in.astype(jnp.float32) + summed
    normed = rms_norm(residual, norm_gain)
    logits = jnp.dot(normed, router_rows, preferred_element_type=jnp.float32)
    hit_mask = expert_ids[:, :, None] == lax.iota(jnp.int32, logits.shape[1])[None, None, :]
    chosen = jnp.sum(jnp.where(hit_mask, logits[:, None, :], 0.0), axis=-1)
    raised = jnp.exp(chosen)
    route_weight = raised / jnp.sum(raised, axis=-1, keepdims=True)
    replica, slot_index = route_block(expert_ids, split_pick, replica_expert)
    within_cap = slot_index < capacity
    buffer_row = jnp.where(within_cap, replica * capacity + slot_index, -1).reshape(-1)
    slot_total = replica_total * capacity
    matches = buffer_row[None, :] == lax.iota(jnp.int32, slot_total)[:, None]
    filled = jnp.any(matches, axis=1)
    row_of_pair = lax.iota(jnp.int32, tok_rows * top_count) // top_count
    anchor = jnp.sum(jnp.where(matches, row_of_pair[None, :], 0), axis=1)
    outgoing = jnp.where(filled[:, None], normed[anchor], jnp.zeros((), jnp.bfloat16))
    outgoing = outgoing.reshape(data_groups, expert_groups, local_reps * capacity, model_width)
    incoming = lax.all_to_all(
        lax.all_to_all(outgoing, "expert", split_axis=1, concat_axis=1, tiled=True),
        "dp",
        split_axis=0,
        concat_axis=0,
        tiled=True,
    )
    results = apply_experts(incoming, up_gate, down, capacity)
    returned = lax.all_to_all(
        lax.all_to_all(results, "dp", split_axis=0, concat_axis=0, tiled=True),
        "expert",
        split_axis=1,
        concat_axis=1,
        tiled=True,
    )
    returned = returned.reshape(slot_total, model_width)
    safe_index = jnp.where(within_cap, replica * capacity + slot_index, 0)
    gathered = returned[safe_index]
    kept_weight = jnp.where(within_cap, route_weight, 0.0)
    layer_out = residual + jnp.sum(kept_weight[:, :, None] * gathered.astype(jnp.float32), axis=1)
    return layer_out.astype(jnp.bfloat16)

MESH = pl.DeviceIdType.MESH
LINE = 4
SIDE = 128
CHUNKS = 4
FAR = LINE + 1
FIRST_LAG = 1
SECOND_LAG = 1
THIRD_LAG = 1
SIDE_LAG = 1
FIRST_LEAD = 1
SECOND_LEAD = 0
ROUTE_ROWS = 32
RING = 4
DOWN_RING = 2
GROUP = 4


def place():
    d, e = lax.axis_index("dp"), lax.axis_index("expert")
    return d // 2, d % 2, e // 2, e % 2


def device_of(y, c, z, x):
    return (y * 2 + c, z * 2 + x)


def block_of(y, c, z, x):
    return (y * 2 + c) * (2 * LINE) + z * 2 + x


def greet(barrier, y, c, z, x):
    for other in (device_of(y, 1 - c, z, x), device_of(1 - y, c, z, x), device_of(y, c, z, 1 - x)):
        pl.semaphore_signal(barrier, inc=1, device_id=other, device_id_type=MESH)

    @pl.when(z > 0)
    def _():
        pl.semaphore_signal(barrier, inc=1, device_id=device_of(y, c, z - 1, x), device_id_type=MESH)

    @pl.when(z < LINE - 1)
    def _():
        pl.semaphore_signal(barrier, inc=1, device_id=device_of(y, c, z + 1, x), device_id_type=MESH)

    pl.semaphore_wait(barrier, 3 + jnp.minimum(z, 1) + jnp.minimum(LINE - 1 - z, 1))


def plane_shift(q, p):
    qa, qb = q & 1, q >> 1
    return qb * (1 - p) + qa * p, qa * (1 - p) + qb * p


def chunk_kind(k):
    return k % 4 == 1, (3 * (k // 4) + (k % 4 + 1) // 2) % 2


def side_kind(k):
    return False, 1


def hops(q, far, m):
    return abs(far - m) + (q & 1) + (q >> 1)


class Place:
    def __init__(self):
        self.y, self.c, self.z, self.x = place()
        self.flip = self.z // 2
        self.m = self.z + self.flip * (LINE - 1 - 2 * self.z)
        self.outward = 1 - 2 * self.flip

    def z_of(self, far):
        return far + self.flip * (LINE - 1 - 2 * far)

    def plane(self, q, p):
        dy, dx = plane_shift(q, p)
        return (self.y + dy) % 2 if dy else self.y, (self.x + dx) % 2 if dx else self.x

    def seat(self, q, far, p):
        y, x = self.plane(q, p)
        return y * (2 * LINE) + self.z_of(far) * 2 + x

    def block(self, q, far, p):
        y, x = self.plane(q, p)
        return block_of(y, self.c, self.z_of(far), x)

    def over(self, q, p):
        y, x = self.plane(q, p)
        return device_of(y, self.c, self.z, x)

    def line(self, way):
        return device_of(self.y, self.c, self.z + way * self.outward, self.x)

    def twin(self):
        return device_of(self.y, 1 - self.c, self.z, self.x)

    def by_class(self, act):
        for m in range(2):
            @pl.when(self.m == m)
            def _(m=m):
                act(m)


def remote(src, dst, send_sem, recv_sem, target):
    return pltpu.make_async_remote_copy(
        src_ref=src, dst_ref=dst, send_sem=send_sem, recv_sem=recv_sem, device_id=target, device_id_type=MESH
    )


class Spread:
    def __init__(self, lag, lead, at, chunks, buf, blocks, kind, line_sem, twin_sem, recv_sem, twin_recv):
        self.at, self.chunks, self.buf, self.blocks, self.kind = at, chunks, buf, blocks, kind
        self.line_sem, self.twin_sem, self.recv_sem, self.twin_recv = line_sem, twin_sem, recv_sem, twin_recv
        self.sent = [0, 0]
        self.lag, self.lead = lag, lead

    def item(self, k, block):
        return self.buf.at[k * self.blocks + block]

    def event(self, k, q, far, m):
        at = self.at
        along_z, p = self.kind(k)
        item, recv = self.item(k, at.block(q, far, p)), self.recv_sem.at[k, at.seat(q, far, p)]
        targets = []
        if q == 0 or along_z:
            if far <= m:
                targets.append(at.line(1))
            if m > 0 and far >= m:
                targets.append(at.line(-1))
        if far == m or not along_z:
            if q <= 1:
                targets.append(at.over(2, p))
            if q == 0:
                targets.append(at.over(1, p))
        if q or far != m:
            remote(item, item, self.line_sem, recv, at.twin()).wait_recv()
        for target in targets:
            remote(item, item, self.line_sem, recv, target).start()
        self.sent[m] += len(targets)

    def twin(self, k, half, core):
        items = self.buf.at[pl.ds(k * self.blocks + (half * 2 + core) * 8, 8)]
        return remote(items, items, self.twin_sem, self.twin_recv.at[k, half], self.at.twin())

    def step(self, s, m):
        for reach in range(LINE + 2):
            for far in range(LINE):
                for q in range(4):
                    k = s - self.lag * reach + (self.lead if reach == 0 else 0)
                    if hops(q, far, m) != reach:
                        continue
                    if reach == 0 and s == 0:
                        for early in range(min(k, self.chunks)):
                            self.event(early, q, far, m)
                    if 0 <= k < self.chunks:
                        self.event(k, q, far, m)
        k = s - self.lag * (FAR - m)
        if 0 <= k < self.chunks:
            for half in range(2):
                self.twin(k, half, self.at.c).start()

    def ready(self, k):
        for half in range(2):
            self.twin(k, half, 1 - self.at.c).wait_recv()

    def drain(self):
        def act(m):
            items = self.buf.at[pl.ds(0, self.sent[m])]
            remote(items, items, self.line_sem, self.recv_sem.at[0, 0], self.at.twin()).wait_send()

        self.at.by_class(act)
        items = self.buf.at[pl.ds(0, self.chunks * 16)]
        remote(items, items, self.twin_sem, self.twin_recv.at[0, 0], self.at.twin()).wait_send()


def layer_kernel(
    plan, hid_ref, ctx_ref, proj_ref, gain_ref, router_ref, ids_ref, rep_ref, split_ref, up_ref, down_ref,
    out_ref, proj_buf, norm_buf, side_buf, weight_side, res_buf, up_ring, down_ring, acc_buf, act_buf, pick_buf,
    place_buf, weight_buf, result_buf, core_buf, a_buf, b_buf, diag_buf, line_buf, line_end, scale_buf, local_sem, up_load,
    down_load, *sems
):
    tok_rows, width, top, capacity, reps, replica_total, expert_total, hidden_units, blocks = plan
    at = Place()
    y, c, z, x = at.y, at.c, at.z, at.x
    me = block_of(y, c, z, x)
    chunk = width // CHUNKS
    groups = blocks // GROUP
    group_rows = GROUP * tok_rows
    seats = GROUP * capacity
    slots = reps * seats
    parts = hidden_units // 2 // chunk
    unit = parts * chunk
    units = width // unit
    f32, bf16 = jnp.float32, jnp.bfloat16

    def own_copy(k):
        return pltpu.make_async_copy(
            proj_ref.at[:, pl.ds(k * chunk, chunk)], proj_buf.at[k * blocks + me], local_sem.at[k]
        )

    def up_copy(i):
        u, j = i // reps, i % reps
        return pltpu.make_async_copy(
            up_ref.at[j, pl.ds(u * unit if isinstance(u, int) else pl.multiple_of(u * unit, unit), unit)], up_ring.at[i % RING], up_load.at[i % RING]
        )

    def down_copy(k):
        return pltpu.make_async_copy(
            down_ref.at[:, :, pl.ds(k * chunk, chunk)],
            down_ring.at[k % DOWN_RING],
            down_load.at[k % DOWN_RING],
        )

    for k in range(CHUNKS):
        own_copy(k).start()
    greet(pltpu.get_barrier_semaphore(), y, c, z, x)
    for i in range(RING):
        up_copy(i).start()
    for k in range(DOWN_RING):
        down_copy(k).start()

    first = Spread(FIRST_LAG, FIRST_LEAD, at, CHUNKS, proj_buf, blocks, chunk_kind, *sems[0:4])
    second = Spread(SECOND_LAG, SECOND_LEAD, at, CHUNKS, norm_buf, blocks, chunk_kind, *sems[4:8])
    first_side = Spread(FIRST_LAG, 0, at, 1, side_buf, blocks, side_kind, *sems[8:12])
    second_side = Spread(SIDE_LAG, 0, at, 1, weight_side, blocks, side_kind, *sems[12:16])
    twin_sem, twin_recv, hop_sem, a_recv, b_recv, diag_recv, line_recv, end_recv = sems[16:]

    for k in range(CHUNKS):
        own_copy(k).wait()
    at.by_class(lambda m: first.step(0, m))

    rep_row = jnp.broadcast_to(rep_ref[...], (replica_total, replica_total))
    row_i = lax.broadcasted_iota(jnp.int32, (replica_total, replica_total), 0)
    col_i = lax.broadcasted_iota(jnp.int32, (replica_total, replica_total), 1)
    rep_col = jnp.sum(jnp.where(row_i == col_i, rep_row, 0), axis=1, keepdims=True)
    rank = jnp.sum(jnp.where((rep_row == rep_col) & (col_i < row_i), 1, 0), axis=1, keepdims=True)
    replica_i = lax.broadcasted_iota(jnp.int32, (replica_total, tok_rows), 0)
    taken = jnp.zeros((replica_total, tok_rows), f32)
    hits, replicas = [], []
    for k in range(top):
        serves = rep_col == ids_ref[k : k + 1, :]
        count = jnp.sum(jnp.where(serves, 1.0, 0.0), axis=0, keepdims=True)
        pick = split_ref[k : k + 1, :].astype(f32)
        wanted = pick - jnp.floor((pick + 0.5) / count) * count
        hit = serves & (rank.astype(f32) == wanted)
        hits.append(hit)
        taken = jnp.where(hit, 1.0, taken)
        replicas.append(jnp.sum(jnp.where(hit, replica_i, 0).astype(f32), axis=0, keepdims=True))
    tok_i = lax.broadcasted_iota(jnp.int32, (tok_rows, tok_rows), 0)
    tok_j = lax.broadcasted_iota(jnp.int32, (tok_rows, tok_rows), 1)
    before = jnp.where(tok_i < tok_j, 1.0, 0.0).astype(bf16)
    earlier = jnp.dot(taken.astype(bf16), before, preferred_element_type=f32)
    slot_rows = [
        jnp.minimum(jnp.sum(jnp.where(hit, earlier, 0.0), axis=0, keepdims=True), float(capacity)) for hit in hits
    ]
    wide_i = lax.broadcasted_iota(jnp.int32, (tok_rows, SIDE), 0)
    wide_j = lax.broadcasted_iota(jnp.int32, (tok_rows, SIDE), 1)
    widen = jnp.where(wide_j == wide_i + x * tok_rows, 1.0, 0.0).astype(bf16)
    routing = jnp.concatenate(replicas + slot_rows, axis=0).astype(bf16)
    side_buf[me, ROUTE_ROWS:] = jnp.dot(routing, widen, preferred_element_type=f32).astype(bf16)
    half_i = lax.broadcasted_iota(jnp.int32, (expert_total, SIDE), 0)
    half_j = lax.broadcasted_iota(jnp.int32, (expert_total, SIDE), 1)
    packed = jnp.zeros((ROUTE_ROWS, SIDE), f32)
    for h in range(2):
        to_half = jnp.where(half_j == half_i + h * expert_total, 1.0, 0.0).astype(bf16)
        packed += jnp.dot(
            router_ref[h * ROUTE_ROWS : (h + 1) * ROUTE_ROWS, :], to_half, preferred_element_type=f32
        )
    side_buf[me, :ROUTE_ROWS] = packed.astype(bf16)

    def project(k):
        first.ready(k)
        weights = proj_buf[k * blocks : (k + 1) * blocks].reshape(width, chunk)
        summed = jnp.dot(ctx_ref[...], weights, preferred_element_type=f32)
        residual = hid_ref[:, k * chunk : (k + 1) * chunk].astype(f32) + summed
        res_buf[k] = residual
        norm_buf[k * blocks + me] = (residual * gain_ref[:, k * chunk : (k + 1) * chunk]).astype(bf16)

    def finish():
        square = jnp.zeros((tok_rows, 1), f32)
        for k in range(CHUNKS):
            square += jnp.sum(res_buf[k] * res_buf[k], axis=1, keepdims=True)
        scale_back = lax.rsqrt(square / width + 1e-05)
        low_logits = jnp.zeros((tok_rows, SIDE), f32)
        high_logits = low_logits
        share = chunk // tok_rows
        in_low = lax.broadcasted_iota(jnp.int32, (tok_rows, chunk), 1) % tok_rows < ROUTE_ROWS
        for k in range(CHUNKS):
            gain = gain_ref[:, k * chunk : (k + 1) * chunk]
            own = (res_buf[k] * scale_back * gain).astype(bf16).astype(f32)
            rows = side_buf[k * share : (k + 1) * share, :ROUTE_ROWS]
            rows = jnp.concatenate([rows, rows], axis=1).reshape(chunk, SIDE)
            low_logits += jnp.dot(jnp.where(in_low, own, 0.0).astype(bf16), rows, preferred_element_type=f32)
            high_logits += jnp.dot(jnp.where(in_low, 0.0, own).astype(bf16), rows, preferred_element_type=f32)
        logits = low_logits.T[:expert_total] + high_logits.T[expert_total:]
        expert_i = lax.broadcasted_iota(jnp.int32, (expert_total, tok_rows), 0)
        raised = [
            jnp.exp(jnp.sum(jnp.where(expert_i == ids_ref[k : k + 1, :], logits, 0.0), axis=0, keepdims=True))
            for k in range(top)
        ]
        raised = jnp.concatenate(raised, axis=0)
        route_weight = raised / jnp.sum(raised, axis=0, keepdims=True)
        upper = route_weight.astype(bf16).astype(f32)
        scale_row = jnp.broadcast_to(scale_back, (tok_rows, SIDE)).T[:1]
        scale_top = scale_row.astype(bf16).astype(f32)
        rest = jnp.zeros((2 * top - 2, tok_rows), f32)
        sent = jnp.concatenate([upper, route_weight - upper, scale_top, scale_row - scale_top, rest], axis=0).astype(bf16)
        weight_side[me] = jnp.dot(sent, widen, preferred_element_type=f32).astype(bf16)

    lane = lax.broadcasted_iota(jnp.int32, (1, group_rows), 1)
    slot_i = lax.broadcasted_iota(jnp.int32, (slots, group_rows), 0).astype(f32)
    seat_base = (lane // tok_rows * capacity).astype(f32)
    low = (me * reps).astype(f32)

    def group_side(ref, g, start, stop):
        def pair(i):
            return ref[GROUP * g + i, start:stop].astype(f32) + ref[GROUP * g + i + 1, start:stop].astype(f32)

        return jnp.concatenate([pair(0), pair(2)], axis=1)

    def seats_of(g):
        routed = group_side(side_buf, g, ROUTE_ROWS, ROUTE_ROWS + 2 * top)
        replica = routed[:top] - low
        slot = routed[top:]
        here = (replica >= 0) & (replica < reps) & (slot < capacity)
        return jnp.where(here, replica * seats + seat_base + slot, -1.0)

    def pick_body(g, carry):
        seat = seats_of(g)
        picked = jnp.zeros((slots, group_rows), f32)
        for k in range(top):
            picked = jnp.where(slot_i == seat[k : k + 1], 1.0, picked)
        pick_buf[g] = picked.astype(bf16)
        place_buf[g] = picked.T.astype(bf16)
        return carry

    def weigh_body(g, carry):
        seat = seats_of(g)
        weights = group_side(weight_side, g, 0, 2 * top)
        weights = weights[:top] + weights[top:]
        weighed = jnp.zeros((slots, group_rows), f32)
        for k in range(top):
            weighed = jnp.where(slot_i == seat[k : k + 1], weights[k : k + 1], weighed)
        weight = jnp.sum(weighed, axis=1, keepdims=True)
        scales = group_side(weight_side, g, 2 * top, 2 * top + 2)
        scale = jnp.sum(pick_buf[g].astype(f32) * (scales[:1] + scales[1:]), axis=1, keepdims=True)
        for j in range(reps):
            rows = pl.ds(pl.multiple_of(g * seats, seats), seats)
            scale_buf[j, rows] = jnp.broadcast_to(scale[j * seats : (j + 1) * seats], (seats, SIDE))
            weight_buf[j, rows] = jnp.broadcast_to(weight[j * seats : (j + 1) * seats], (seats, SIDE))
        return carry

    def take(k):
        second.ready(k)

        def body(g, carry):
            rows = norm_buf[pl.ds(k * blocks + g * GROUP, GROUP)].reshape(group_rows, chunk)
            taken = jnp.dot(pick_buf[g], rows, preferred_element_type=f32).astype(bf16)
            for j in range(reps):
                act_buf[
                    (k // parts % 2) * reps + j,
                    pl.ds(pl.multiple_of(g * seats, seats), seats),
                    (k % parts) * chunk : (k % parts + 1) * chunk,
                ] = taken[j * seats : (j + 1) * seats]
            return carry

        lax.fori_loop(0, groups, body, 0, unroll=True)

    def activate(j):
        scale = scale_buf[j, :, :1]
        for h in range(2):
            half = hidden_units // 2
            gate = acc_buf[j, :, h * half : (h + 1) * half] * scale
            raised = acc_buf[j, :, hidden_units + h * half : hidden_units + (h + 1) * half] * scale
            act_buf[2 * j + h] = (gate / (1.0 + jnp.exp(-gate)) * raised).astype(bf16)

    def raise_some(u, start, stop):
        depth = slice(start * chunk, stop * chunk)

        last = u == units - 1 and stop == parts

        def body(j, carry):
            i = u * reps + j
            if last and j:
                activate(j - 1)
            if start == 0:
                up_copy(i).wait()
            expert_in = act_buf[(u % 2) * reps + j, :, depth]
            for t in range(4):
                columns = slice(t * (2 * hidden_units // 4), (t + 1) * (2 * hidden_units // 4))
                acc_buf[j, :, columns] += jnp.dot(
                    expert_in, up_ring[i % RING, depth, columns], preferred_element_type=f32
                )
            if stop == parts and u < units - 1:
                up_copy(i + RING).start()
            return carry

        if last:
            for j in range(reps):
                body(j, 0)
            activate(reps - 1)
        else:
            lax.fori_loop(0, reps, body, 0)

    def raise_after(k):
        u, part = k // parts, k % parts
        if u == units - 1:
            raise_some(u, part, part + 1)
        elif part == parts - 1:
            raise_some(u, 0, parts)

    acc_buf[...] = jnp.zeros_like(acc_buf)
    begin = FIRST_LAG * FAR + 1
    known = begin + CHUNKS
    used = begin + SECOND_LAG * FAR + 1
    side_end = known + SIDE_LAG * FAR
    assert side_end <= used + CHUNKS - 1
    for s in range(1, used + CHUNKS):
        def gather_step(m, s=s):
            first.step(s, m)
            first_side.step(s - 1, m)

        at.by_class(gather_step)
        if begin <= s < begin + CHUNKS:
            project(s - begin)
        at.by_class(lambda m, s=s: second.step(s - begin, m))
        if s == begin + 1:
            first_side.ready(0)
            lax.fori_loop(0, groups, pick_body, 0)
        if s == known - 1:
            finish()
        at.by_class(lambda m, s=s: second_side.step(s - known + 1, m))
        if used <= s < used + CHUNKS:
            take(s - used)
            if s == used + CHUNKS - 1:
                second_side.ready(0)
                lax.fori_loop(0, groups, weigh_body, 0, unroll=2)
            raise_after(s - used)

    first.drain()
    first_side.drain()

    def lower_chunk(k):
        down_copy(k).wait()
        for j in range(reps):
            half = hidden_units // 2
            result = jnp.dot(act_buf[2 * j], down_ring[k % DOWN_RING, j, :half], preferred_element_type=f32)
            result += jnp.dot(act_buf[2 * j + 1], down_ring[k % DOWN_RING, j, half:], preferred_element_type=f32)
            result = (result * weight_buf[j, :, :1]).astype(bf16)
            for g in range(groups):
                some = result[g * seats : (g + 1) * seats]
                result_buf[g, j * seats : (j + 1) * seats] = some

        if k + DOWN_RING < CHUNKS:
            down_copy(k + DOWN_RING).start()

        def body(g, carry):
            summed = jnp.dot(place_buf[g], result_buf[g], preferred_element_type=f32).astype(bf16)
            proj_buf[pl.ds(k * blocks + g * GROUP, GROUP)] = summed.reshape(GROUP, tok_rows, chunk)
            return carry

        lax.fori_loop(0, groups, body, 0, unroll=True)

    def to_twin(k, half):
        return remote(
            proj_buf.at[pl.ds(k * blocks + (half * 2 + 1 - c) * 8, 8)],
            core_buf.at[pl.ds(k * 16 + half * 8, 8)],
            twin_sem,
            twin_recv.at[k, half],
            at.twin(),
        )

    def line_slot(k, q, far):
        before = sum(4 * LINE if chunk_kind(i)[0] else LINE for i in range(k))
        return before + q * LINE + at.z_of(far)

    def end_slot(k, q):
        return sum(4 if chunk_kind(i)[0] else 1 for i in range(k)) + q

    hop_count = [0, 0]

    def join(k, q, far, m):
        along_z, p = chunk_kind(k)
        target_z = at.z_of(far)
        in_plane = far == m or not along_z
        children = []
        if q == 1 and in_plane:
            children.append((diag_buf.at[k * LINE + target_z], diag_recv.at[k, target_z]))
        if q == 0 and in_plane:
            children.append((a_buf.at[k * LINE + target_z], a_recv.at[k, target_z]))
            children.append((b_buf.at[k * LINE + target_z], b_recv.at[k, target_z]))
        if q == 0 or along_z:
            if far <= m or m > 0:
                slot = line_slot(k, q, far)
                children.append((line_buf.at[slot], line_recv.at[slot]))
            if far == m and m > 0:
                slot = end_slot(k, q)
                children.append((line_end.at[slot], end_recv.at[slot]))
        held = core_buf.at[k * 16 + at.seat(q, far, p)]
        for ref, sem in children:
            remote(ref, ref, hop_sem, sem, at.twin()).wait_recv()
        total = held[...].astype(f32) + proj_buf[k * blocks + at.block(q, far, p)].astype(f32)
        for ref, _ in children:
            total += ref[...].astype(f32)
        if q == 0 and far == m:
            out_ref[:, k * chunk : (k + 1) * chunk] = (res_buf[k] + total).astype(bf16)
            return
        held[...] = total.astype(bf16)
        if q and in_plane:
            buf, sem = {1: (a_buf, a_recv), 2: (b_buf, b_recv), 3: (diag_buf, diag_recv)}[q]
            dst, recv = buf.at[k * LINE + target_z], sem.at[k, target_z]
            target = at.over(1 if q == 1 else 2, p)
        else:
            target = at.line(1 if far > m else -1)
            if m == 0 and far == 1:
                slot = end_slot(k, q)
                dst, recv = line_end.at[slot], end_recv.at[slot]
            else:
                slot = line_slot(k, q, far)
                dst, recv = line_buf.at[slot], line_recv.at[slot]
        remote(held, dst, hop_sem, recv, target).start()
        hop_count[m] += 1

    def join_step(s, m):
        for reach in range(LINE + 1, -1, -1):
            for q in (3, 1, 2, 0):
                for far in range(LINE - 1, -1, -1):
                    for k in range(CHUNKS):
                        if hops(q, far, m) == reach and s - 1 == k + THIRD_LAG * (FAR - reach):
                            join(k, q, far, m)

    for s in range(CHUNKS + THIRD_LAG * FAR + 1):
        if s < CHUNKS:
            lower_chunk(s)
            for half in range(2):
                to_twin(s, half).start()
        if 1 <= s <= CHUNKS:
            for half in range(2):
                to_twin(s - 1, half).wait_recv()
        at.by_class(lambda m: join_step(s, m))

    def hop_drain(m):
        items = core_buf.at[pl.ds(0, hop_count[m])]
        remote(items, items, hop_sem, a_recv.at[0, 0], at.twin()).wait_send()

    at.by_class(hop_drain)
    items = core_buf.at[pl.ds(0, CHUNKS * 16)]
    remote(items, items, twin_sem, twin_recv.at[0, 0], at.twin()).wait_send()
    second.drain()
    second_side.drain()


def run_layer(
    hidden_in, context, out_proj, norm_gain, router, expert_ids, replica_expert, split_pick, up_gate, down
):
    tok_rows, width = hidden_in.shape
    top = expert_ids.shape[1]
    replica_total = replica_expert.shape[0]
    expert_total = router.shape[1]
    reps, hidden_units, _ = down.shape
    blocks = lax.axis_size("dp") * lax.axis_size("expert")
    capacity = max(2, 2 * tok_rows * top // replica_total)
    chunk = width // CHUNKS
    groups = blocks // GROUP
    seats = GROUP * capacity
    slots = reps * seats
    dma = pltpu.SemaphoreType.DMA
    vmem, anywhere = pl.BlockSpec(memory_space=pltpu.VMEM), pl.BlockSpec(memory_space=pl.ANY)

    def spread_sems(chunks):
        return [dma, dma, dma((chunks, 16)), dma((chunks, 2))]

    lines = sum(4 if chunk_kind(k)[0] else 1 for k in range(CHUNKS))
    bf16, f32 = jnp.bfloat16, jnp.float32
    plan = (tok_rows, width, top, capacity, reps, replica_total, expert_total, hidden_units, blocks)
    return pl.pallas_call(
        functools.partial(layer_kernel, plan),
        out_shape=jax.ShapeDtypeStruct((tok_rows, width), bf16),
        in_specs=[vmem, vmem, anywhere, vmem, vmem, vmem, vmem, vmem, anywhere, anywhere],
        out_specs=vmem,
        scratch_shapes=[
            pltpu.VMEM((CHUNKS * blocks, tok_rows, chunk), bf16),
            pltpu.VMEM((CHUNKS * blocks, tok_rows, chunk), bf16),
            pltpu.VMEM((blocks, ROUTE_ROWS + 2 * top, SIDE), bf16),
            pltpu.VMEM((blocks, 4 * top, SIDE), bf16),
            pltpu.VMEM((CHUNKS, tok_rows, chunk), f32),
            pltpu.VMEM((RING, hidden_units // 2, 2 * hidden_units), bf16),
            pltpu.VMEM((DOWN_RING, reps, hidden_units, chunk), bf16),
            pltpu.VMEM((reps, groups * seats, 2 * hidden_units), f32),
            pltpu.VMEM((2 * reps, groups * seats, hidden_units // 2), bf16),
            pltpu.VMEM((groups, slots, GROUP * tok_rows), bf16),
            pltpu.VMEM((groups, GROUP * tok_rows, slots), bf16),
            pltpu.VMEM((reps, groups * seats, SIDE), f32),
            pltpu.VMEM((groups, slots, chunk), bf16),
            pltpu.VMEM((CHUNKS * 16, tok_rows, chunk), bf16),
            pltpu.VMEM((CHUNKS * LINE, tok_rows, chunk), bf16),
            pltpu.VMEM((CHUNKS * LINE, tok_rows, chunk), bf16),
            pltpu.VMEM((CHUNKS * LINE, tok_rows, chunk), bf16),
            pltpu.VMEM((lines * LINE, tok_rows, chunk), bf16),
            pltpu.VMEM((lines, tok_rows, chunk), bf16),
            pltpu.VMEM((reps, groups * seats, SIDE), f32),
            dma((CHUNKS,)),
            dma((RING,)),
            dma((DOWN_RING,)),
        ]
        + spread_sems(CHUNKS)
        + spread_sems(CHUNKS)
        + spread_sems(1)
        + spread_sems(1)
        + [
            dma,
            dma((CHUNKS, 2)),
            dma,
            dma((CHUNKS, LINE)),
            dma((CHUNKS, LINE)),
            dma((CHUNKS, LINE)),
            dma((lines * LINE,)),
            dma((lines,)),
        ],
        compiler_params=pltpu.CompilerParams(collective_id=0, has_side_effects=True, vmem_limit_bytes=62 << 20),
    )(
        hidden_in, context, out_proj, norm_gain.reshape(1, width), router, expert_ids.T,
        replica_expert.reshape(1, replica_total), split_pick.T, up_gate, down,
    )


def solution(mesh):
    plan = run_layer if (mesh.shape["dp"], mesh.shape["expert"]) == (4, 8) else per_device
    return jax.shard_map(
        plan,
        mesh=mesh,
        in_specs=(
            P(("dp", "expert"), None),
            P(("dp", "expert"), None),
            P(("dp", "expert"), None),
            P(),
            P(("dp", "expert"), None),
            P(("dp", "expert"), None),
            P(),
            P(("dp", "expert"), None),
            P(("dp", "expert"), None, None),
            P(("dp", "expert"), None, None),
        ),
        out_specs=P(("dp", "expert"), None),
        check_vma=False,
    )
```
